256 devices in a mesh: kx: 32 (over z, x), ky: 8 (over y, core).
Axes of the slice: x: 4, y: 4, z: 8, core: 2. Of those that a mesh axis runs over, the one named last changes fastest.
Arguments:
- slip_rate: float32 [3, 2048, 2048], P(None, ('kx', 'ky')), may hold values from -6 to 6
- slip_field: float32 [3, 2048, 2048], P(None, ('kx', 'ky')), may hold values from -6 to 6
- prestress: float32 [3, 2048, 2048], P(None, ('kx', 'ky')), may hold values from -6 to 6
- history: bfloat16 [6, 3, 2, 2048, 2048], P(None, None, None, ('kx', 'ky')), may hold values from -6 to 6
- kernel: float32 [8, 8, 3], replicated, may hold values from -3 to 3
- band_len: int32 [8], replicated, may hold values from 2 to 8, as said below
- mode_band: int32 [2048, 2048], P(('kx', 'ky')), may hold values from 0 to 7
Outputs:
- new_rate: float32 [3, 2048, 2048], P(None, ('kx', 'ky'))
- new_slip: float32 [3, 2048, 2048], P(None, ('kx', 'ky'))
The draws below stay inside these ranges and needn't reach their ends.
Inputs may be any that keep to these rules, and one draw needn't show every extreme that they name: `band_len`: entry 0 equals 8; every other entry lies between 2 and 4.
All inputs are finite; a program needn't handle non-finite values.
Results may differ from the reference program's by a relative error of at most 0.0003.
Values sent between devices are 32-bit elements; how exact they have to be, the bound alone decides.
A program may use at most 128 MiB of HBM per device.

```python
import jax
import jax.numpy as jnp

NX = 2048
NY = 2048
BANDS = 8
LAGS = 8
STEPS = 1
HIST = 6


def draw_band_len(key, part):
    others = jax.random.randint(key, (BANDS,), 2, LAGS // 2 + 1)
    position = jnp.arange(BANDS, dtype=jnp.int32)
    return jnp.where(position == 0, LAGS, others).astype(jnp.int32)


def draw_mode_band(key, part):
    ymode = jnp.arange(NY, dtype=jnp.int32)[:, None]
    xmode = jnp.arange(NX, dtype=jnp.int32)[None, :]
    ysigned = jnp.where(ymode < NY // 2, ymode, ymode - NY)
    xsigned = jnp.where(xmode < NX // 2, xmode, xmode - NX)
    radius_sq = xsigned * xsigned + ysigned * ysigned
    base = jnp.zeros((NY, NX), jnp.int32)
    for band_index in range(1, BANDS):
        threshold = max(NX * NY // 4 ** (BANDS + 1 - band_index), 1)
        base = base + (radius_sq >= threshold).astype(jnp.int32)
    jitter = jax.random.randint(key, (NY, NX), 0, 3) - 1
    return jnp.clip(base + jitter, 0, BANDS - 1).astype(jnp.int32)


def shard_levels(stream_key, dims, shards, least, largest):
    loudness, own = 1.0, jax.random.fold_in(stream_key, 6)
    for axis_at, parts in shards:
        heights = jnp.exp(jax.random.uniform(jax.random.fold_in(own, axis_at), (parts,), jnp.float32, least / len(shards), largest / len(shards)))
        loudness = loudness * jnp.repeat(heights, dims[axis_at] // parts).reshape([-1 if axis == axis_at else 1 for axis in range(len(dims))])
    return loudness


def gaussian(rng, dims, scale, reach, cuts=(), held_as=jnp.bfloat16):
    result = scale * jax.random.normal(rng, dims, jnp.float32)
    if cuts:
        result = result * shard_levels(rng, dims, cuts, -0.22, 0.18)
    return jnp.clip(result, -reach, reach).astype(held_as)


def setup_inputs(seed: int = 0) -> dict:
    key_of = jax.random.split(jax.random.key(seed), 8)
    slip_rate = gaussian(key_of[0], (3, NX, NY), 1.0, 6.0, ((1, 256),), jnp.float32)
    slip_field = gaussian(key_of[1], (3, NX, NY), 1.0, 6.0, ((1, 256),), jnp.float32)
    prestress = gaussian(key_of[2], (3, NX, NY), 1.0, 6.0, ((1, 256),), jnp.float32)
    history = gaussian(key_of[3], (HIST, 3, 2, NY, NX), 1.0, 6.0, ((3, 256),))
    kernel = gaussian(key_of[4], (BANDS, LAGS, 3), 0.5, 3.0, (), jnp.float32)
    band_len = draw_band_len(jax.random.fold_in(key_of[7], 71), 0)
    mode_band = draw_mode_band(jax.random.fold_in(key_of[7], 71), 0)
    return {"slip_rate": slip_rate, "slip_field": slip_field, "prestress": prestress, "history": history, "kernel": kernel, "band_len": band_len, "mode_band": mode_band}


static_fric = 0.7
dynamic_fric = 0.35
weaken_slip = 0.5

def friction(stress, total):
    worn = jnp.sqrt(total[0] * total[0] + total[1] * total[1] + 1.0) - 1.0
    coeff = dynamic_fric + (static_fric - dynamic_fric) * jnp.exp(-worn / weaken_slip)
    strength = coeff * jax.nn.softplus(-stress[2])
    magnitude = jnp.sqrt(stress[0] * stress[0] + stress[1] * stress[1] + 1.0)
    glide = jax.nn.softplus(magnitude - strength)
    return jnp.stack([glide * stress[0] / magnitude, glide * stress[1] / magnitude, jax.nn.softplus(stress[2])])

def lag_weights(kernel, band_len, mode_band, lag_index):
    live = (lag_index < band_len).astype(jnp.float32)
    table = kernel[:, lag_index, :] * live[:, None]
    picked = table[mode_band]
    return jnp.transpose(picked, (2, 0, 1))[:, None]

def spectrum(field_real):
    whole = jnp.fft.fft2(field_real, norm='ortho')
    whole = jnp.transpose(whole, (0, 2, 1))
    return jnp.stack([jnp.real(whole), jnp.imag(whole)], axis=1).astype(jnp.float32)

def surface(spectra):
    whole = spectra[:, 0] + 1j * spectra[:, 1]
    whole = jnp.transpose(whole, (0, 2, 1))
    return jnp.real(jnp.fft.ifft2(whole, norm='ortho')).astype(jnp.float32)

def reference(slip_rate, slip_field, prestress, history, kernel, band_len, mode_band):
    computed = [spectrum(slip_rate)]
    speed = slip_rate
    total = slip_field
    for step_index in range(STEPS):
        carried = jnp.zeros_like(computed[0])
        for lag_index in range(1, LAGS):
            weight = lag_weights(kernel, band_len, mode_band, lag_index)
            if lag_index <= len(computed):
                source = computed[lag_index - 1]
            else:
                source = history[lag_index - len(computed) - 1].astype(jnp.float32)
            carried = carried + weight * source
        now = computed[0]
        instant = lag_weights(kernel, band_len, mode_band, 0)
        first_rate = friction(prestress + surface(carried + instant * now), total)
        tried = 0.5 * (now + spectrum(first_rate))
        second_rate = friction(prestress + surface(carried + instant * tried), total)
        total = total + 0.25 * (speed + second_rate)
        speed = second_rate
        if step_index + 1 < STEPS:
            computed = [spectrum(speed)] + computed
    return (speed, total)
```

```python
import functools

import jax
import jax.numpy as jnp
import numpy as np
from jax import lax
from jax.experimental import pallas as pl
from jax.experimental.pallas import tpu as pltpu
from jax.sharding import PartitionSpec as P

MESH = pl.DeviceIdType.MESH
N = 2048
DEV = 256
SLOTS = 5
BANDS = 8
LAGS = 8
F32 = jnp.float32
BF16 = jnp.bfloat16


def split(table):
    table = np.asarray(table, np.float64)
    high = table.astype(np.float32).astype(jnp.bfloat16)
    low = (table - high.astype(np.float64)).astype(np.float32).astype(jnp.bfloat16)
    return np.stack([np.asarray(high), np.asarray(low)])


def lane(slot, comp, at):
    return slot * 24 + comp * 8 + at


@functools.cache
def tables():
    scale = 1.0 / np.sqrt(N)
    k2, n2 = np.arange(256)[:, None], np.arange(512)[None, :]
    angle = 2 * np.pi / 512 * (k2 * n2 % 512)
    y_table = split(np.concatenate([np.cos(angle), np.sin(angle)], 1) * scale)
    k1, s = np.arange(256)[:, None], np.arange(256)[None, :]
    angle = 2 * np.pi / 256 * (k1 * s % 256)
    x_table = split(np.concatenate([np.cos(angle), np.sin(angle)], 1) * scale)
    slots = np.arange(8)[:, None]
    angle = 2 * np.pi / N * (slots * n2 % N)
    y_twist = np.stack([np.cos(angle), np.sin(angle)]).astype(np.float32)
    x_twist = np.zeros((2, 256, 128), np.float32)
    eight = np.arange(8)
    for slot in range(SLOTS):
        for comp in range(3):
            at = lane(slot, comp, 0)
            angle = 2 * np.pi / N * (np.arange(256)[:, None] * eight[None, :])
            x_twist[0, :, at : at + 8] = np.cos(angle)
            x_twist[1, :, at : at + 8] = np.sin(angle)
    angle = 2 * np.pi / 8 * (eight[:, None] * eight[None, :] % 8)
    cos8, sin8 = np.cos(angle), np.sin(angle)
    forward = np.zeros((256, 256))
    inverse = np.zeros((256, 256))
    for slot in range(SLOTS):
        for comp in range(3):
            at = lane(slot, comp, 0)
            re, im = slice(at, at + 8), slice(128 + at, 128 + at + 8)
            forward[re, re], forward[im, re] = cos8, sin8
            forward[re, im], forward[im, im] = -sin8, cos8
            inverse[re, re], inverse[im, re] = cos8, -sin8
            inverse[re, im], inverse[im, im] = sin8, cos8
    eights = np.stack([split(forward), split(inverse)])
    own_rows = [{0: 0, 1: 1, 2: 2, 3: 3}, {0: 4, 1: 3, 2: 2, 3: 1, 4: 0}]
    sent_rows = [{0: 4, 1: 5, 2: 6, 3: 7}, {1: 7, 2: 6, 3: 5}]
    past = np.zeros((2, 384, 512))
    for half in range(2):
        for block, rows in enumerate((own_rows[half], sent_rows[half])):
            for slot, row in rows.items():
                for comp in range(3):
                    out = block * 256 + lane(slot, comp, 0)
                    re, im = slice(out, out + 8), slice(out + 128, out + 136)
                    for mode in range(8):
                        in_re = ((comp * 2 + 0) * 8 + mode) * 8 + row
                        in_im = ((comp * 2 + 1) * 8 + mode) * 8 + row
                        past[half, in_re, re] = cos8[mode]
                        past[half, in_im, re] = -sin8[mode]
                        past[half, in_re, im] = sin8[mode]
                        past[half, in_im, im] = cos8[mode]
    past = np.stack([split(past[0]), split(past[1])])
    picks = np.zeros((2, 3, 128, 128), np.float32)
    missing = np.full((2, 2, 8, 128), 8.0, np.float32)
    plain = [{slot: (0, slot) for slot in range(4)}, {slot: (1, 4 + slot) for slot in range(4)}]
    turned = [{slot: (1, 8 - slot) for slot in (1, 2, 3)}, {slot: (0, 4 - slot) for slot in range(5)}]
    for half in range(2):
        for kind, (which, source) in enumerate(
            ((plain, eight), (turned, 7 - eight), (turned, (8 - eight) % 8))
        ):
            for slot, (block, row) in which[half].items():
                for comp in range(3):
                    for mode in range(8):
                        out = lane(slot, comp, mode)
                        picks[half, kind, (block * 8 + source[mode]) * 8 + row, out] = 1.0
                        missing[half, min(kind, 1), :, out] = 0.0
    picks = picks.astype(jnp.bfloat16)
    turn = np.zeros((256, 256), np.float32)
    turn[np.arange(256), (256 - np.arange(256)) % 256] = 1.0
    turn = turn.astype(jnp.bfloat16)
    return y_table, x_table, y_twist, x_twist, eights, past, picks, missing, turn


def halves(value):
    high = value.astype(BF16)
    low = (value - high.astype(F32)).astype(BF16)
    return high, low


NN = (((1,), (0,)), ((), ()))
NT = (((1,), (1,)), ((), ()))


def product(left, right, dims=NN):
    (left_high, left_low), (right_high, right_low) = left, right
    dot = functools.partial(lax.dot_general, dimension_numbers=dims, preferred_element_type=F32)
    return dot(left_high, right_high) + (dot(left_high, right_low) + dot(left_low, right_high))


def softplus(value):
    return jnp.maximum(value, 0.0) + jnp.log1p(jnp.exp(-jnp.abs(value)))


def block_of(device):
    return 2 * device + (device // 128) * (511 - 4 * device)


def body(
    slip_rate, slip_field, prestress, history, mode_band,
    y_table, x_table, y_twist, x_twist, eights, past, picks, missing, turn,
    kern, band_len,
    new_rate, new_slip,
    send, recv, stacked, bands, given, taken, partner_band,
    send_sem, recv_sem, pair_send, pair_recv, own_sem,
):
    kx, ky = lax.axis_index("kx"), lax.axis_index("ky")
    me = kx * 8 + ky
    half = me // 128
    mine = block_of(me)
    partner = 255 - me
    partner_id = (partner // 8, lax.rem(partner, 8))

    barrier = pltpu.get_barrier_semaphore()

    def greet(step, carry):
        other = lax.rem(me + step, DEV)
        pl.semaphore_signal(
            barrier, inc=1, device_id=(other // 8, lax.rem(other, 8)), device_id_type=MESH
        )
        return carry

    lax.fori_loop(1, DEV, greet, 0)

    def exchange(turn_at, forward):
        def one(device):
            if forward:
                source, target = send.at[turn_at, block_of(device)], recv.at[turn_at, me]
            else:
                source, target = send.at[turn_at, device], recv.at[turn_at, mine]
            pltpu.make_async_remote_copy(
                source, target, send_sem.at[turn_at], recv_sem.at[turn_at],
                device_id=(device // 8, lax.rem(device, 8)), device_id_type=MESH,
            ).start()

        one(lax.rem(me + 128, DEV))

        def two(step, carry):
            one(lax.rem(me + 128 + step, DEV))
            one(lax.rem(me + 128 - step, DEV))
            return carry

        lax.fori_loop(1, 128, two, 0)
        if forward:
            source, target = send.at[turn_at, mine], recv.at[turn_at, me]
        else:
            source, target = send.at[turn_at, me], recv.at[turn_at, mine]
        pltpu.make_async_copy(source, target, recv_sem.at[turn_at]).start()

    def arrive(turn_at):
        whole = recv.at[turn_at]
        pltpu.make_async_copy(whole, whole, recv_sem.at[turn_at]).wait()
        gone = send.at[turn_at, pl.ds(0, DEV - 1)]
        pltpu.make_async_copy(gone, gone, send_sem.at[turn_at]).wait()

    def put(turn_at, re, im):
        send[turn_at, :, 0, :] = re
        send[turn_at, :, 1, :] = im

    def y_forward(field):
        cos, sin = y_twist[0], y_twist[1]
        re_rows, im_rows = [[] for _ in range(SLOTS)], [[] for _ in range(SLOTS)]
        for comp in range(3):
            part = [field[comp][:, 512 * n : 512 * (n + 1)] for n in range(4)]
            even, odd = part[0] + part[2], part[1] + part[3]
            left, right = part[0] - part[2], part[1] - part[3]
            pairs = [(even + odd, None), (left, -right), (even - odd, None), (left, right), (even + odd, None)]
            for slot, (re, im) in enumerate(pairs):
                c, s = cos[slot : slot + 1], sin[slot : slot + 1]
                if slot == 0:
                    re_rows[slot].append(re)
                    im_rows[slot].append(jnp.zeros_like(re))
                elif im is None:
                    re_rows[slot].append(re * c)
                    im_rows[slot].append(-(re * s))
                else:
                    re_rows[slot].append(re * c + im * s)
                    im_rows[slot].append(im * c - re * s)
        pad = jnp.zeros((8, 512), F32)
        re = jnp.concatenate(sum(re_rows, []) + [pad], 0)
        im = jnp.concatenate(sum(im_rows, []) + [pad], 0)
        re_high, re_low = halves(re)
        im_high, im_low = halves(im)

        def arrange(r, i):
            return jnp.concatenate([jnp.concatenate([r, i], 1), jnp.concatenate([i, -r], 1)], 0)

        out = product(
            (y_table[0], y_table[1]), (arrange(re_high, im_high), arrange(re_low, im_low)), NT
        )
        return out[:, :128], out[:, 128:]

    def y_inverse(turn_at):
        re = halves(recv[turn_at, :, 0, :].T)
        im = halves(recv[turn_at, :, 1, :].T)

        def arrange(r, i):
            return jnp.concatenate([jnp.concatenate([r, -i], 1), jnp.concatenate([i, r], 1)], 0)

        def tall(n):
            return jnp.concatenate([y_table[n, :, :512], y_table[n, :, 512:]], 0)

        out = product((arrange(re[0], im[0]), arrange(re[1], im[1])), (tall(0), tall(1)))
        cos, sin = y_twist[0], y_twist[1]

        def turned(slot, comp, want_im):
            a = out[lane(slot, comp, 0) : lane(slot, comp, 8)]
            if slot == 0:
                return a, None
            b = out[128 + lane(slot, comp, 0) : 128 + lane(slot, comp, 8)]
            c, s = cos[slot : slot + 1], sin[slot : slot + 1]
            return a * c - b * s, (b * c + a * s) if want_im else None

        field = []
        for comp in range(3):
            base = turned(0, comp, False)[0] + turned(4, comp, False)[0]
            one_re, one_im = turned(1, comp, True)
            two_re, _ = turned(2, comp, False)
            three_re, three_im = turned(3, comp, True)
            up, down = base + two_re, base - two_re
            re_sum, im_dif = one_re + three_re, one_im - three_im
            field.append([up + re_sum, down - im_dif, up - re_sum, down + im_dif])
        return field

    def x_transform(re, im, sign):
        re_high, re_low = halves(re)
        im_high, im_low = halves(im)

        def arrange(r, i):
            if sign < 0:
                return jnp.concatenate([jnp.concatenate([r, i], 1), jnp.concatenate([i, -r], 1)], 0)
            return jnp.concatenate([jnp.concatenate([r, i], 1), jnp.concatenate([-i, r], 1)], 0)

        out = product(
            (x_table[0], x_table[1]), (arrange(re_high, im_high), arrange(re_low, im_low))
        )
        return out[:, :128], out[:, 128:]

    def twist(re, im, sign):
        cos, sin = x_twist[0], x_twist[1]
        if sign < 0:
            return re * cos + im * sin, im * cos - re * sin
        return re * cos - im * sin, im * cos + re * sin

    def x_forward(turn_at):
        re, im = x_transform(recv[turn_at, :, 0, :], recv[turn_at, :, 1, :], -1)
        re, im = twist(re, im, -1)
        out = product(halves(jnp.concatenate([re, im], 1)), (eights[0, 0], eights[0, 1]))
        return out[:, :128], out[:, 128:]

    def x_inverse(re, im):
        out = product(halves(jnp.concatenate([re, im], 1)), (eights[1, 0], eights[1, 1]))
        re, im = twist(out[:, :128], out[:, 128:], 1)
        return x_transform(re, im, 1)

    put(0, *y_forward([slip_rate[comp] for comp in range(3)]))
    pl.semaphore_wait(barrier, DEV - 1)
    exchange(0, True)
    band_copy = pltpu.make_async_remote_copy(
        mode_band, partner_band, pair_send.at[0], pair_recv.at[0],
        device_id=partner_id, device_id_type=MESH,
    )
    band_copy.start()

    def live(band, lag, comp):
        kept = (band_len[band] > lag).astype(F32)
        return kern[(band * LAGS + lag) * 3 + comp] * kept

    effective = {
        (band, lag, comp): live(band, lag, comp)
        for lag in (0, 1, 2, 3) for comp in range(3) for band in range(BANDS)
    }
    effective.update({(0, lag, comp): live(0, lag, comp) for lag in range(4, LAGS) for comp in range(3)})

    def gather(mode, carry):
        at = pl.multiple_of(mode * 256, 256)
        band = mode_band[:, pl.ds(at, 256)]
        chosen = [band == b for b in range(BANDS)]
        for comp in range(3):
            total = [jnp.zeros((8, 256), F32), jnp.zeros((8, 256), F32)]
            for lag in range(2, LAGS):
                weight = jnp.zeros((8, 256), F32)
                for b in range(BANDS if lag < 4 else 1):
                    weight = jnp.where(chosen[b], effective[b, lag, comp], weight)
                for part in range(2):
                    source = history[lag - 2, comp, part, :, pl.ds(at, 256)].astype(F32)
                    total[part] = total[part] + weight * source
            for part in range(2):
                row = pl.multiple_of(((comp * 2 + part) * 8 + mode) * 8, 8)
                stacked[pl.ds(row, 8), :] = total[part]
        row = pl.multiple_of(mode * 8, 8)
        bands[pl.ds(row, 8), :] = band.astype(F32)
        return carry

    lax.fori_loop(0, 8, gather, 0)
    flat = halves(stacked[...].T)
    out = product(flat, (past[half, 0], past[half, 1]))
    given_re, given_im = x_transform(*twist(out[:, 256:384], out[:, 384:], 1), 1)
    given[0] = given_re
    given[1] = given_im
    given_copy = pltpu.make_async_remote_copy(
        given, taken, pair_send.at[1], pair_recv.at[1],
        device_id=partner_id, device_id_type=MESH,
    )
    given_copy.start()
    own_re, own_im = x_transform(*twist(out[:, :128], out[:, 128:256], 1), 1)

    band_copy.wait()
    for mode in range(8):
        bands[64 + mode * 8 : 72 + mode * 8, :] = partner_band[:, mode * 256 : (mode + 1) * 256].astype(F32)
    plain = bands[...].T.astype(BF16)
    dot = functools.partial(lax.dot_general, dimension_numbers=NN, preferred_element_type=F32)
    turned = dot(turn[...], plain).astype(BF16)
    first_row = lax.broadcasted_iota(jnp.int32, (256, 128), 0) == 0
    plain_band = dot(plain, picks[half, 0]) + missing[half, 0, 0:1]
    turned_band = (
        jnp.where(first_row, dot(turned, picks[half, 2]), dot(turned, picks[half, 1]))
        + missing[half, 1, 0:1]
    )
    lane_at = lax.broadcasted_iota(jnp.int32, (1, 128), 1)
    lane_comp = lax.rem(lane_at // 8, 3)
    weight = [jnp.zeros((256, 128), F32) for _ in range(2)]
    for which in (plain_band, turned_band):
        chosen = [jnp.zeros((256, 128), F32) for _ in range(2)]
        for b in range(BANDS):
            hit = which == float(b)
            for lag in range(2):
                value = jnp.where(
                    lane_comp == 0, effective[b, lag, 0],
                    jnp.where(lane_comp == 1, effective[b, lag, 1], effective[b, lag, 2]),
                )
                chosen[lag] = jnp.where(hit, value, chosen[lag])
        weight = [weight[lag] + chosen[lag] for lag in range(2)]
    first_weight = weight[0] + weight[1]
    now_weight = weight[1] + 0.5 * weight[0]
    tried_weight = 0.5 * weight[0]

    given_copy.wait()
    sign = 1.0 - 2.0 * half.astype(F32)
    held_re = own_re + taken[0]
    held_im = sign * (own_im - taken[1])

    slip = [slip_field[comp] for comp in range(2)]
    worn = jnp.sqrt(slip[0] * slip[0] + slip[1] * slip[1] + 1.0) - 1.0
    coeff = 0.35 + 0.35 * jnp.exp(worn * -2.0)

    def slide(field, write):
        rates = [[], [], []]
        for n in range(4):
            part = slice(512 * n, 512 * (n + 1))
            s = [prestress[comp, :, part] + field[comp][n] for comp in range(3)]
            strength = coeff[:, part] * softplus(-s[2])
            magnitude = jnp.sqrt(s[0] * s[0] + s[1] * s[1] + 1.0)
            ratio = softplus(magnitude - strength) / magnitude
            for comp, value in enumerate((ratio * s[0], ratio * s[1], softplus(s[2]))):
                if write:
                    new_rate[comp, :, part] = value
                    new_slip[comp, :, part] = slip_field[comp, :, part] + 0.25 * (
                        slip_rate[comp, :, part] + value
                    )
                rates[comp].append(value)
        return [jnp.concatenate(rate, 1) for rate in rates]

    arrive(0)
    now_re, now_im = x_forward(0)
    re, im = x_inverse(now_re * first_weight, now_im * first_weight)
    put(1, re + held_re, im + held_im)
    exchange(1, False)
    re, im = x_inverse(now_re * now_weight, now_im * now_weight)
    given[0] = re + held_re
    given[1] = im + held_im
    arrive(1)
    first = slide(y_inverse(1), False)

    put(2, *y_forward(first))
    exchange(2, True)
    arrive(2)
    re, im = x_forward(2)
    re, im = x_inverse(re * tried_weight, im * tried_weight)
    put(3, re + given[0], im + given[1])
    exchange(3, False)
    arrive(3)
    slide(y_inverse(3), True)


def on_device(slip_rate, slip_field, prestress, history, kernel, band_len, mode_band):
    vmem = pl.BlockSpec(memory_space=pltpu.VMEM)
    smem = pl.BlockSpec(memory_space=pltpu.SMEM)
    constants = [jnp.asarray(table) for table in tables()]
    shape = jax.ShapeDtypeStruct((3, 8, N), F32)
    dma = pltpu.SemaphoreType.DMA
    return pl.pallas_call(
        body,
        out_shape=(shape, shape),
        in_specs=[vmem] * (5 + len(constants)) + [smem] * 2,
        out_specs=(vmem, vmem),
        scratch_shapes=[
            pltpu.VMEM((4, DEV, 2, 128), F32),
            pltpu.VMEM((4, DEV, 2, 128), F32),
            pltpu.VMEM((384, 256), F32),
            pltpu.VMEM((128, 256), F32),
            pltpu.VMEM((2, 256, 128), F32),
            pltpu.VMEM((2, 256, 128), F32),
            pltpu.VMEM((8, N), jnp.int32),
            dma((4,)), dma((4,)), dma((2,)), dma((2,)), dma((1,)),
        ],
        compiler_params=pltpu.CompilerParams(
            collective_id=0, has_side_effects=True, vmem_limit_bytes=56 * 1024 * 1024
        ),
    )(slip_rate, slip_field, prestress, history, mode_band, *constants, kernel.reshape(-1), band_len)


def solution(mesh):
    rows = P(None, ("kx", "ky"), None)
    return jax.shard_map(
        on_device,
        mesh=mesh,
        in_specs=(
            rows, rows, rows, P(None, None, None, ("kx", "ky"), None), P(), P(), P(("kx", "ky"), None),
        ),
        out_specs=(rows, rows),
        check_vma=False,
    )
```

```python
import functools

import jax
import jax.numpy as jnp
import numpy as np
from jax import lax
from jax.experimental import pallas as pl
from jax.experimental.pallas import tpu as pltpu
from jax.sharding import PartitionSpec as P

MESH = pl.DeviceIdType.MESH
N = 2048
DEV = 256
SLOTS = 5
BANDS = 8
LAGS = 8
F32 = jnp.float32
BF16 = jnp.bfloat16


def split(table):
    table = np.asarray(table, np.float64)
    high = table.astype(np.float32).astype(jnp.bfloat16)
    low = (table - high.astype(np.float64)).astype(np.float32).astype(jnp.bfloat16)
    return np.stack([np.asarray(high), np.asarray(low)])


def lane(slot, comp, at):
    return slot * 24 + comp * 8 + at


@functools.cache
def tables():
    scale = 1.0 / np.sqrt(N)
    k2, n2 = np.arange(256)[:, None], np.arange(512)[None, :]
    angle = 2 * np.pi / 512 * (k2 * n2 % 512)
    y_table = split(np.concatenate([np.cos(angle), np.sin(angle)], 1) * scale)
    k1, s = np.arange(256)[:, None], np.arange(256)[None, :]
    angle = 2 * np.pi / 256 * (k1 * s % 256)
    x_table = split(np.concatenate([np.cos(angle), np.sin(angle)], 1) * scale)
    slots = np.arange(8)[:, None]
    angle = 2 * np.pi / N * (slots * n2 % N)
    y_twist = np.stack([np.cos(angle), np.sin(angle)]).astype(np.float32)
    x_twist = np.zeros((2, 256, 128), np.float32)
    eight = np.arange(8)
    for group in range(16):
        angle = 2 * np.pi / N * (np.arange(256)[:, None] * eight[None, :])
        x_twist[0, :, group * 8 : group * 8 + 8] = np.cos(angle)
        x_twist[1, :, group * 8 : group * 8 + 8] = np.sin(angle)
    angle = 2 * np.pi / 8 * (eight[:, None] * eight[None, :] % 8)
    cos8, sin8 = np.cos(angle), np.sin(angle)
    forward = np.zeros((256, 256))
    inverse = np.zeros((256, 256))
    for slot in range(SLOTS):
        for comp in range(3):
            at = lane(slot, comp, 0)
            re, im = slice(at, at + 8), slice(128 + at, 128 + at + 8)
            forward[re, re], forward[im, re] = cos8, sin8
            forward[re, im], forward[im, im] = -sin8, cos8
            inverse[re, re], inverse[im, re] = cos8, -sin8
            inverse[re, im], inverse[im, im] = sin8, cos8
    eights = np.stack([split(forward), split(inverse)])
    past = np.zeros((2, 384, 512))

    def fill(table, out_re, out_im, comp, row, turned):
        re, im = slice(out_re, out_re + 8), slice(out_im, out_im + 8)
        for mode in range(8):
            in_re = ((comp * 2 + 0) * 8 + mode) * 8 + row
            in_im = ((comp * 2 + 1) * 8 + mode) * 8 + row
            if turned:
                table[in_re, re], table[in_im, re] = sin8[mode], cos8[mode]
                table[in_re, im], table[in_im, im] = -cos8[mode], sin8[mode]
            else:
                table[in_re, re], table[in_im, re] = cos8[mode], -sin8[mode]
                table[in_re, im], table[in_im, im] = sin8[mode], cos8[mode]

    for half, (own, other) in enumerate((((0, 1, 2, 3, 4), (5, 6, 7)), ((4, 3, 2, 1, 0), (7, 6, 5)))):
        for slot, row in enumerate(own):
            for comp in range(3):
                at = lane(slot, comp, 0)
                fill(past[half], at, 128 + at, comp, row, False)
        for slot, row in enumerate(other):
            for comp in range(3):
                group = slot * 3 + comp
                if group == 8:
                    fill(past[half], 120, 248, comp, row, False)
                else:
                    at = 256 + group * 8
                    fill(past[half], at, 128 + at, comp, row, False)
                    fill(past[half], at + 64, 192 + at, comp, row, True)
    past = np.stack([split(past[0]), split(past[1])])
    picks = np.zeros((2, 3, 128, 128), np.float32)
    missing = np.full((2, 2, 8, 128), 8.0, np.float32)
    plain = [{slot: (0, slot) for slot in range(4)}, {slot: (1, 4 + slot) for slot in range(4)}]
    turned = [{slot: (1, 8 - slot) for slot in (1, 2, 3)}, {slot: (0, 4 - slot) for slot in range(5)}]
    for half in range(2):
        for kind, (which, source) in enumerate(
            ((plain, eight), (turned, 7 - eight), (turned, (8 - eight) % 8))
        ):
            for slot, (block, row) in which[half].items():
                for comp in range(3):
                    for mode in range(8):
                        out = lane(slot, comp, mode)
                        picks[half, kind, (block * 8 + source[mode]) * 8 + row, out] = 1.0
                        missing[half, min(kind, 1), :, out] = 0.0
    picks = picks.astype(jnp.bfloat16)
    turn = np.zeros((256, 256), np.float32)
    turn[np.arange(256), (256 - np.arange(256)) % 256] = 1.0
    turn = turn.astype(jnp.bfloat16)
    return y_table, x_table, y_twist, x_twist, eights, past, picks, missing, turn


def halves(value):
    high = value.astype(BF16)
    low = (value - high.astype(F32)).astype(BF16)
    return high, low


NN = (((1,), (0,)), ((), ()))
NT = (((1,), (1,)), ((), ()))


def product(left, right, dims=NN):
    (left_high, left_low), (right_high, right_low) = left, right
    dot = functools.partial(lax.dot_general, dimension_numbers=dims, preferred_element_type=F32)
    return dot(left_high, right_high) + (dot(left_high, right_low) + dot(left_low, right_high))


def softplus(value):
    return jnp.maximum(value, 0.0) + jnp.log1p(jnp.exp(-jnp.abs(value)))


def block_of(device):
    return 2 * device + (device // 128) * (511 - 4 * device)


def slide(stress, coeff):
    strength = coeff * softplus(-stress[2])
    magnitude = jnp.sqrt(stress[0] * stress[0] + stress[1] * stress[1] + 1.0)
    ratio = softplus(magnitude - strength) / magnitude
    return ratio * stress[0], ratio * stress[1], softplus(stress[2])


def weakening(first, second):
    worn = jnp.sqrt(first * first + second * second + 1.0) - 1.0
    return 0.35 + 0.35 * jnp.exp(worn * -2.0)


def body(
    slip_rate_in, slip_field_in, prestress_in, history_in, mode_band_in,
    y_table_in, x_table_in, y_twist_in, x_twist_in, eights_in, past_in, picks_in, missing_in, turn_in,
    kern, band_len,
    stress_out,
    slip_rate, slip_field, prestress, history, mode_band,
    y_table, x_table, y_twist, x_twist, eights, past, picks, missing, turn,
    send_0, send_1, send_2, send_3, recv_0, recv_1, recv_2, recv_3,
    stacked, bands, hold, kept, partner_band,
    send_sem, recv_sem, pair_send, pair_recv, load_sem,
):
    kx, ky = lax.axis_index("kx"), lax.axis_index("ky")
    me = kx * 8 + ky
    half = me // 128
    mine = block_of(me)
    partner = 255 - me
    partner_id = (partner // 8, lax.rem(partner, 8))
    send, recv = (send_0, send_1, send_2, send_3), (recv_0, recv_1, recv_2, recv_3)

    partner_band[0:4] = jnp.zeros((4, N), jnp.int32)
    loads = {}
    for at, (name, source, target) in enumerate((
        ("slip_rate", slip_rate_in, slip_rate),
        ("y_twist", y_twist_in, y_twist),
        ("y_table", y_table_in, y_table),
        ("mode_band", mode_band_in, mode_band),
        ("history", history_in, history),
        ("past", past_in.at[half], past),
        ("x_twist", x_twist_in, x_twist),
        ("x_table", x_table_in, x_table),
        ("turn", turn_in, turn),
        ("picks", picks_in.at[half], picks),
        ("missing", missing_in.at[half], missing),
        ("eights", eights_in, eights),
        ("slip_field", slip_field_in, slip_field),
        ("prestress", prestress_in, prestress),
    )):
        loads[name] = pltpu.make_async_copy(source, target, load_sem.at[at])
        loads[name].start()

    barrier = pltpu.get_barrier_semaphore()

    def greet(step, carry):
        other = lax.rem(me + step, DEV)
        pl.semaphore_signal(
            barrier, inc=1, device_id=(other // 8, lax.rem(other, 8)), device_id_type=MESH
        )
        return carry

    lax.fori_loop(1, DEV, greet, 0, unroll=5)

    def exchange(turn_at, forward):
        def one(device):
            if forward:
                source, target = send[turn_at].at[block_of(device)], recv[turn_at].at[me]
            else:
                source, target = send[turn_at].at[device], recv[turn_at].at[mine]
            pltpu.make_async_remote_copy(
                source, target, send_sem.at[turn_at], recv_sem.at[turn_at],
                device_id=(device // 8, lax.rem(device, 8)), device_id_type=MESH,
            ).start()

        one(lax.rem(me + 128, DEV))
        one(lax.rem(me + 129, DEV))
        one(lax.rem(me + 127, DEV))

        def two(step, carry):
            one(lax.rem(me + 128 + step, DEV))
            one(lax.rem(me + 128 - step, DEV))
            return carry

        lax.fori_loop(2, 128, two, 0, unroll=7)
        if forward:
            source, target = send[turn_at].at[mine], recv[turn_at].at[me]
        else:
            source, target = send[turn_at].at[me], recv[turn_at].at[mine]
        pltpu.make_async_copy(source, target, recv_sem.at[turn_at]).start()

    def arrive(turn_at):
        whole = recv[turn_at]
        pltpu.make_async_copy(whole, whole, recv_sem.at[turn_at]).wait()

    def sent(turn_at):
        gone = send[turn_at].at[pl.ds(0, DEV - 1)]
        pltpu.make_async_copy(gone, gone, send_sem.at[turn_at]).wait()

    def put(turn_at, *rows):
        for at, row in enumerate(rows):
            send[turn_at][:, at, :] = row

    def y_forward(field):
        cos, sin = y_twist[0], y_twist[1]
        re_rows, im_rows = [[] for _ in range(SLOTS)], [[] for _ in range(SLOTS)]
        for comp in range(3):
            part = [field[comp][:, 512 * n : 512 * (n + 1)] for n in range(4)]
            even, odd = part[0] + part[2], part[1] + part[3]
            left, right = part[0] - part[2], part[1] - part[3]
            pairs = [(even + odd, None), (left, -right), (even - odd, None), (left, right), (even + odd, None)]
            for slot, (re, im) in enumerate(pairs):
                c, s = cos[slot : slot + 1], sin[slot : slot + 1]
                if slot == 0:
                    re_rows[slot].append(re)
                    im_rows[slot].append(jnp.zeros_like(re))
                elif im is None:
                    re_rows[slot].append(re * c)
                    im_rows[slot].append(-(re * s))
                else:
                    re_rows[slot].append(re * c + im * s)
                    im_rows[slot].append(im * c - re * s)
        pad = jnp.zeros((8, 512), F32)
        re = jnp.concatenate(sum(re_rows, []) + [pad], 0)
        im = jnp.concatenate(sum(im_rows, []) + [pad], 0)
        re_high, re_low = halves(re)
        im_high, im_low = halves(im)

        def arrange(r, i):
            return jnp.concatenate([jnp.concatenate([r, i], 1), jnp.concatenate([i, -r], 1)], 0)

        out = product(
            (y_table[0], y_table[1]), (arrange(re_high, im_high), arrange(re_low, im_low)), NT
        )
        return out[:, :128], out[:, 128:]

    def swap(value):
        even = lax.rem(lax.broadcasted_iota(jnp.int32, value.shape, 1), 2) == 0
        return jnp.where(even, pltpu.roll(value, 255, 1), pltpu.roll(value, 1, 1))

    def y_inverse(turn_at):
        re = recv[turn_at][:, 0, :].T
        im = recv[turn_at][:, 1, :].T
        if turn_at == 1:
            rest = recv[turn_at][:, 2, :].T
            kept[0] = swap(jnp.concatenate([rest[0:64], re[120:128]], 0))
            kept[1] = swap(jnp.concatenate([rest[64:128], im[120:128]], 0))
        re = halves(jnp.concatenate([re[:24], re[24:96] + kept[0], re[96:]], 0))
        im = halves(jnp.concatenate([im[:24], im[24:96] + kept[1], im[96:]], 0))

        def arrange(r, i):
            return jnp.concatenate([jnp.concatenate([r, -i], 1), jnp.concatenate([i, r], 1)], 0)

        def tall(n):
            return jnp.concatenate([y_table[n, :, :512], y_table[n, :, 512:]], 0)

        out = product((arrange(re[0], im[0]), arrange(re[1], im[1])), (tall(0), tall(1)))
        cos, sin = y_twist[0], y_twist[1]

        def turned(slot, comp, want_im):
            a = out[lane(slot, comp, 0) : lane(slot, comp, 8)]
            if slot == 0:
                return a, None
            b = out[128 + lane(slot, comp, 0) : 128 + lane(slot, comp, 8)]
            c, s = cos[slot : slot + 1], sin[slot : slot + 1]
            return a * c - b * s, (b * c + a * s) if want_im else None

        field = []
        for comp in range(3):
            base = turned(0, comp, False)[0] + turned(4, comp, False)[0]
            one_re, one_im = turned(1, comp, True)
            two_re, _ = turned(2, comp, False)
            three_re, three_im = turned(3, comp, True)
            up, down = base + two_re, base - two_re
            re_sum, im_dif = one_re + three_re, one_im - three_im
            field.append([up + re_sum, down - im_dif, up - re_sum, down + im_dif])
        return field

    def x_transform(re, im, sign):
        re_high, re_low = halves(re)
        im_high, im_low = halves(im)

        def arrange(r, i):
            if sign < 0:
                return jnp.concatenate([jnp.concatenate([r, i], 1), jnp.concatenate([i, -r], 1)], 0)
            return jnp.concatenate([jnp.concatenate([r, i], 1), jnp.concatenate([-i, r], 1)], 0)

        out = product(
            (x_table[0], x_table[1]), (arrange(re_high, im_high), arrange(re_low, im_low))
        )
        return out[:, :128], out[:, 128:]

    def twist(re, im, sign):
        cos, sin = x_twist[0], x_twist[1]
        if sign < 0:
            return re * cos + im * sin, im * cos - re * sin
        return re * cos - im * sin, im * cos + re * sin

    def x_forward(turn_at):
        re, im = x_transform(recv[turn_at][:, 0, :], recv[turn_at][:, 1, :], -1)
        re, im = twist(re, im, -1)
        out = product(halves(jnp.concatenate([re, im], 1)), (eights[0, 0], eights[0, 1]))
        return out[:, :128], out[:, 128:]

    def x_inverse(re, im):
        out = product(halves(jnp.concatenate([re, im], 1)), (eights[1, 0], eights[1, 1]))
        re, im = twist(out[:, :128], out[:, 128:], 1)
        return x_transform(re, im, 1)

    for name in ("slip_rate", "y_twist", "y_table"):
        loads[name].wait()
    put(0, *y_forward([slip_rate[comp] for comp in range(3)]))

    def live(band, lag, comp):
        kept = (band_len[band] > lag).astype(F32)
        return kern[comp, band, lag] * kept

    effective = {
        (band, lag, comp): live(band, lag, comp)
        for lag in (0, 1, 2, 3) for comp in range(3) for band in range(BANDS)
    }
    effective.update({(0, lag, comp): live(0, lag, comp) for lag in range(4, LAGS) for comp in range(3)})

    for name in ("mode_band", "history", "past", "x_twist", "x_table"):
        loads[name].wait()

    def gather(mode, carry):
        at = pl.multiple_of(mode * 256, 256)
        band = mode_band[:, pl.ds(at, 256)]
        chosen = [band == b for b in range(BANDS)]
        for comp in range(3):
            total = [jnp.zeros((8, 256), F32), jnp.zeros((8, 256), F32)]
            for lag in range(2, LAGS):
                weight = jnp.zeros((8, 256), F32)
                for b in range(BANDS if lag < 4 else 1):
                    weight = jnp.where(chosen[b], effective[b, lag, comp], weight)
                for part in range(2):
                    source = history[lag - 2, comp, part, :, pl.ds(at, 256)].astype(F32)
                    total[part] = total[part] + weight * source
            for part in range(2):
                row = pl.multiple_of(((comp * 2 + part) * 8 + mode) * 8, 8)
                stacked[pl.ds(row, 8), :] = total[part]
        row = pl.multiple_of(mode * 8, 8)
        bands[pl.ds(row, 8), :] = band.astype(F32)
        return carry

    lax.fori_loop(0, 8, gather, 0)
    flat = halves(stacked[...].T)
    out = product(flat, (past[0], past[1]))
    sign = 1.0 - 2.0 * half.astype(F32)
    held_re, held_im = x_transform(*twist(out[:, :128], out[:, 128:256], 1), 1)
    hold[0] = held_re
    hold[1] = held_im * sign
    rest_re, rest_im = twist(out[:, 256:384], out[:, 384:], 1)
    rest_re, rest_im = halves(rest_re), halves(rest_im)
    rest = product(
        (x_table[0], x_table[1]),
        tuple(jnp.concatenate([rest_re[n], -rest_im[n]], 0) for n in range(2)),
    )
    lane_at = lax.broadcasted_iota(jnp.int32, (1, 128), 1)
    send_1[:, 2, :] = rest * jnp.where(lane_at < 64, 1.0, sign)

    pl.semaphore_wait(barrier, DEV - 1)
    band_copy = pltpu.make_async_remote_copy(
        mode_band.at[pl.ds(4, 4)], partner_band.at[pl.ds(4, 4)], pair_send.at[0], pair_recv.at[0],
        device_id=partner_id, device_id_type=MESH,
    )
    band_copy.start()
    exchange(0, True)
    for name in ("turn", "picks", "missing", "eights", "slip_field", "prestress"):
        loads[name].wait()

    band_copy.wait()
    for mode in range(8):
        bands[64 + mode * 8 : 72 + mode * 8, :] = partner_band[:, mode * 256 : (mode + 1) * 256].astype(F32)
    plain = bands[...].T.astype(BF16)
    dot = functools.partial(lax.dot_general, dimension_numbers=NN, preferred_element_type=F32)
    turned = dot(turn[...], plain).astype(BF16)
    first_row = lax.broadcasted_iota(jnp.int32, (256, 128), 0) == 0
    plain_band = dot(plain, picks[0]) + missing[0, 0:1]
    turned_band = (
        jnp.where(first_row, dot(turned, picks[2]), dot(turned, picks[1]))
        + missing[1, 0:1]
    )
    lane_comp = lax.rem(lane_at // 8, 3)
    weight = [jnp.zeros((256, 128), F32) for _ in range(2)]
    for which in (plain_band, turned_band):
        chosen = [jnp.zeros((256, 128), F32) for _ in range(2)]
        for b in range(BANDS):
            hit = which == float(b)
            for lag in range(2):
                value = jnp.where(
                    lane_comp == 0, effective[b, lag, 0],
                    jnp.where(lane_comp == 1, effective[b, lag, 1], effective[b, lag, 2]),
                )
                chosen[lag] = jnp.where(hit, value, chosen[lag])
        weight = [weight[lag] + chosen[lag] for lag in range(2)]
    first_weight = weight[0] + weight[1]
    now_weight = weight[1] + 0.5 * weight[0]
    tried_weight = 0.5 * weight[0]

    coeff = weakening(slip_field[0], slip_field[1])

    arrive(0)
    now_re, now_im = x_forward(0)
    re, im = x_inverse(now_re * first_weight, now_im * first_weight)
    put(1, re + hold[0], im + hold[1])
    exchange(1, False)
    re, im = x_inverse(now_re * now_weight, now_im * now_weight)
    hold[0] = re + hold[0]
    hold[1] = im + hold[1]
    arrive(1)
    field = y_inverse(1)
    stress = [prestress[comp] + jnp.concatenate(field[comp], 1) for comp in range(3)]

    put(2, *y_forward(slide(stress, coeff)))
    exchange(2, True)
    arrive(2)
    re, im = x_forward(2)
    re, im = x_inverse(re * tried_weight, im * tried_weight)
    put(3, re + hold[0], im + hold[1])
    exchange(3, False)
    arrive(3)
    field = y_inverse(3)
    for comp in range(3):
        for n in range(4):
            part = slice(512 * n, 512 * (n + 1))
            stress_out[comp, :, part] = prestress[comp, :, part] + field[comp][n]
    for turn_at in range(4):
        sent(turn_at)


def finish(stress, slip_field, slip_rate, new_rate, new_slip):
    coeff = weakening(slip_field[0], slip_field[1])
    for comp, value in enumerate(slide([stress[comp] for comp in range(3)], coeff)):
        new_rate[comp] = value
        new_slip[comp] = slip_field[comp] + 0.25 * (slip_rate[comp] + value)


def on_device(slip_rate, slip_field, prestress, history, kernel, band_len, mode_band):
    vmem = pl.BlockSpec(memory_space=pltpu.VMEM)
    smem = pl.BlockSpec(memory_space=pltpu.SMEM)
    anywhere = pl.BlockSpec(memory_space=pltpu.HBM)
    constants = [jnp.asarray(table) for table in tables()]
    halved = (5, 6, 7)
    shape = jax.ShapeDtypeStruct((3, 8, N), F32)
    dma = pltpu.SemaphoreType.DMA
    inputs = (slip_rate, slip_field, prestress, history, mode_band)
    stress = pl.pallas_call(
        body,
        out_shape=shape,
        in_specs=[anywhere] * (5 + len(constants)) + [smem] * 2,
        out_specs=vmem,
        scratch_shapes=[
            *[pltpu.VMEM(value.shape, value.dtype) for value in inputs],
            *[
                pltpu.VMEM(value.shape[1:] if at in halved else value.shape, value.dtype)
                for at, value in enumerate(constants)
            ],
            *[pltpu.VMEM((DEV, 3 if at == 1 else 2, 128), F32) for at in (0, 1, 2, 3)] ,
            *[pltpu.VMEM((DEV, 3 if at == 1 else 2, 128), F32) for at in (0, 1, 2, 3)],
            pltpu.VMEM((384, 256), F32),
            pltpu.VMEM((128, 256), F32),
            pltpu.VMEM((2, 256, 128), F32),
            pltpu.VMEM((2, 72, 256), F32),
            pltpu.VMEM((8, N), jnp.int32),
            dma((4,)), dma((4,)), dma((1,)), dma((1,)), dma((14,)),
        ],
        compiler_params=pltpu.CompilerParams(
            collective_id=0, has_side_effects=True, vmem_limit_bytes=67043328
        ),
    )(*inputs, *constants, jnp.transpose(kernel, (2, 0, 1)), band_len)
    return pl.pallas_call(
        finish, out_shape=(shape, shape), in_specs=[vmem] * 3, out_specs=(vmem, vmem)
    )(stress, slip_field, slip_rate)


def solution(mesh):
    rows = P(None, ("kx", "ky"), None)
    return jax.shard_map(
        on_device,
        mesh=mesh,
        in_specs=(
            rows, rows, rows, P(None, None, None, ("kx", "ky"), None), P(), P(), P(("kx", "ky"), None),
        ),
        out_specs=(rows, rows),
        check_vma=False,
    )
```

```python
import functools

import jax
import jax.numpy as jnp
import numpy as np
from jax import lax
from jax.experimental import pallas as pl
from jax.experimental.pallas import tpu as pltpu
from jax.sharding import PartitionSpec as P

MESH = pl.DeviceIdType.MESH
N = 2048
DEV = 256
SLOTS = 5
BANDS = 8
LAGS = 8
F32 = jnp.float32
BF16 = jnp.bfloat16


def split(table):
    table = np.asarray(table, np.float64)
    high = table.astype(np.float32).astype(jnp.bfloat16)
    low = (table - high.astype(np.float64)).astype(np.float32).astype(jnp.bfloat16)
    return np.stack([np.asarray(high), np.asarray(low)])


def lane(slot, comp, at):
    return slot * 24 + comp * 8 + at


@functools.cache
def tables():
    scale = 1.0 / np.sqrt(N)
    k2, n2 = np.arange(256)[:, None], np.arange(512)[None, :]
    angle = 2 * np.pi / 512 * (k2 * n2 % 512)
    y_table = split(np.concatenate([np.cos(angle), np.sin(angle)], 1) * scale)
    k1, s = np.arange(256)[:, None], np.arange(256)[None, :]
    angle = 2 * np.pi / 256 * (k1 * s % 256)
    x_table = split(np.concatenate([np.cos(angle), np.sin(angle)], 1) * scale)
    slots = np.arange(8)[:, None]
    angle = 2 * np.pi / N * (slots * n2 % N)
    y_twist = np.stack([np.cos(angle), np.sin(angle)]).astype(np.float32)
    x_twist = np.zeros((2, 256, 128), np.float32)
    eight = np.arange(8)
    for group in range(16):
        angle = 2 * np.pi / N * (np.arange(256)[:, None] * eight[None, :])
        x_twist[0, :, group * 8 : group * 8 + 8] = np.cos(angle)
        x_twist[1, :, group * 8 : group * 8 + 8] = np.sin(angle)
    angle = 2 * np.pi / 8 * (eight[:, None] * eight[None, :] % 8)
    cos8, sin8 = np.cos(angle), np.sin(angle)
    forward = np.zeros((256, 256))
    inverse = np.zeros((256, 256))
    for slot in range(SLOTS):
        for comp in range(3):
            at = lane(slot, comp, 0)
            re, im = slice(at, at + 8), slice(128 + at, 128 + at + 8)
            forward[re, re], forward[im, re] = cos8, sin8
            forward[re, im], forward[im, im] = -sin8, cos8
            inverse[re, re], inverse[im, re] = cos8, -sin8
            inverse[re, im], inverse[im, im] = sin8, cos8
    eights = np.stack([split(forward), split(inverse)])
    past = np.zeros((2, 384, 512))

    def fill(table, out_re, out_im, comp, row, turned):
        re, im = slice(out_re, out_re + 8), slice(out_im, out_im + 8)
        for mode in range(8):
            in_re = ((comp * 2 + 0) * 8 + mode) * 8 + row
            in_im = ((comp * 2 + 1) * 8 + mode) * 8 + row
            if turned:
                table[in_re, re], table[in_im, re] = sin8[mode], cos8[mode]
                table[in_re, im], table[in_im, im] = -cos8[mode], sin8[mode]
            else:
                table[in_re, re], table[in_im, re] = cos8[mode], -sin8[mode]
                table[in_re, im], table[in_im, im] = sin8[mode], cos8[mode]

    for half, (own, other) in enumerate((((0, 1, 2, 3, 4), (5, 6, 7)), ((4, 3, 2, 1, 0), (7, 6, 5)))):
        for slot, row in enumerate(own):
            for comp in range(3):
                at = lane(slot, comp, 0)
                fill(past[half], at, 128 + at, comp, row, False)
        for slot, row in enumerate(other):
            for comp in range(3):
                group = slot * 3 + comp
                if group == 8:
                    fill(past[half], 120, 248, comp, row, False)
                else:
                    at = 256 + group * 8
                    fill(past[half], at, 128 + at, comp, row, False)
                    fill(past[half], at + 64, 192 + at, comp, row, True)
    past = np.stack([split(past[0]), split(past[1])])
    picks = np.zeros((2, 3, 128, 128), np.float32)
    missing = np.full((2, 2, 8, 128), 8.0, np.float32)
    plain = [{slot: (0, slot) for slot in range(4)}, {slot: (1, 4 + slot) for slot in range(4)}]
    turned = [{slot: (1, 8 - slot) for slot in (1, 2, 3)}, {slot: (0, 4 - slot) for slot in range(5)}]
    for half in range(2):
        for kind, (which, source) in enumerate(
            ((plain, eight), (turned, 7 - eight), (turned, (8 - eight) % 8))
        ):
            for slot, (block, row) in which[half].items():
                for comp in range(3):
                    for mode in range(8):
                        out = lane(slot, comp, mode)
                        picks[half, kind, (block * 8 + source[mode]) * 8 + row, out] = 1.0
                        missing[half, min(kind, 1), :, out] = 0.0
    picks = picks.astype(jnp.bfloat16)
    turn = np.zeros((256, 256), np.float32)
    turn[np.arange(256), (256 - np.arange(256)) % 256] = 1.0
    turn = turn.astype(jnp.bfloat16)
    return y_table, x_table, y_twist, x_twist, eights, past, picks, missing, turn


def halves(value):
    high = value.astype(BF16)
    low = (value - high.astype(F32)).astype(BF16)
    return high, low


NN = (((1,), (0,)), ((), ()))
NT = (((1,), (1,)), ((), ()))


def product(left, right, dims=NN):
    (left_high, left_low), (right_high, right_low) = left, right
    dot = functools.partial(lax.dot_general, dimension_numbers=dims, preferred_element_type=F32)
    return dot(left_high, right_high) + (dot(left_high, right_low) + dot(left_low, right_high))


def softplus(value):
    return jnp.maximum(value, 0.0) + jnp.log1p(jnp.exp(-jnp.abs(value)))


def block_of(device):
    return 2 * device + (device // 128) * (511 - 4 * device)


def slide(stress, coeff):
    strength = coeff * softplus(-stress[2])
    magnitude = jnp.sqrt(stress[0] * stress[0] + stress[1] * stress[1] + 1.0)
    ratio = softplus(magnitude - strength) / magnitude
    return ratio * stress[0], ratio * stress[1], softplus(stress[2])


def weakening(first, second):
    worn = jnp.sqrt(first * first + second * second + 1.0) - 1.0
    return 0.35 + 0.35 * jnp.exp(worn * -2.0)


def body(
    slip_rate_in, slip_field_in, prestress_in, history_in, mode_band_in,
    y_table_in, x_table_in, y_twist_in, x_twist_in, eights_in, past_in, picks_in, missing_in, turn_in,
    kern, band_len,
    stress_out,
    slip_rate, slip_field, prestress, history, mode_band,
    y_table, x_table, y_twist, x_twist, eights, past, picks, missing, turn,
    send_0, send_1, send_2, send_3, send_4, recv_0, recv_1, recv_2, recv_3, recv_4,
    stacked, bands, hold, kept, partner_band,
    send_sem, recv_sem, pair_send, pair_recv, load_sem,
):
    kx, ky = lax.axis_index("kx"), lax.axis_index("ky")
    me = kx * 8 + ky
    half = me // 128
    mine = block_of(me)
    partner = 255 - me
    partner_id = (partner // 8, lax.rem(partner, 8))
    send = (send_0, send_1, send_2, send_3, send_4)
    recv = (recv_0, recv_1, recv_2, recv_3, recv_4)

    partner_band[0:4] = jnp.zeros((4, N), jnp.int32)
    loads = {}
    for at, (name, source, target) in enumerate((
        ("slip_rate", slip_rate_in, slip_rate),
        ("y_twist", y_twist_in, y_twist),
        ("y_table", y_table_in, y_table),
        ("mode_band", mode_band_in, mode_band),
        ("history", history_in, history),
        ("past", past_in.at[half], past),
        ("x_twist", x_twist_in, x_twist),
        ("x_table", x_table_in, x_table),
        ("turn", turn_in, turn),
        ("picks", picks_in.at[half], picks),
        ("missing", missing_in.at[half], missing),
        ("eights", eights_in, eights),
        ("slip_field", slip_field_in, slip_field),
        ("prestress", prestress_in, prestress),
    )):
        loads[name] = pltpu.make_async_copy(source, target, load_sem.at[at])
        loads[name].start()

    barrier = pltpu.get_barrier_semaphore()

    def greet(other):
        pl.semaphore_signal(
            barrier, inc=1, device_id=(other // 8, lax.rem(other, 8)), device_id_type=MESH
        )

    def greet_two(step, carry):
        greet(lax.rem(me + 128 + step, DEV))
        greet(lax.rem(me + 128 - step, DEV))
        return carry

    greet(lax.rem(me + 128, DEV))
    greet(lax.rem(me + 129, DEV))
    greet(lax.rem(me + 127, DEV))
    lax.fori_loop(2, 128, greet_two, 0, unroll=7)

    def exchange(turn_at, forward):
        def one(device):
            if forward:
                source, target = send[turn_at].at[block_of(device)], recv[turn_at].at[me]
            else:
                source, target = send[turn_at].at[device], recv[turn_at].at[mine]
            pltpu.make_async_remote_copy(
                source, target, send_sem.at[turn_at], recv_sem.at[turn_at],
                device_id=(device // 8, lax.rem(device, 8)), device_id_type=MESH,
            ).start()

        one(lax.rem(me + 128, DEV))
        one(lax.rem(me + 129, DEV))
        one(lax.rem(me + 127, DEV))

        def two(step, carry):
            one(lax.rem(me + 128 + step, DEV))
            one(lax.rem(me + 128 - step, DEV))
            return carry

        lax.fori_loop(2, 128, two, 0, unroll=7)
        if forward:
            source, target = send[turn_at].at[mine], recv[turn_at].at[me]
        else:
            source, target = send[turn_at].at[me], recv[turn_at].at[mine]
        pltpu.make_async_copy(source, target, recv_sem.at[turn_at]).start()

    def arrive(turn_at):
        whole = recv[turn_at]
        pltpu.make_async_copy(whole, whole, recv_sem.at[turn_at]).wait()

    def sent(turn_at):
        gone = send[turn_at].at[pl.ds(0, DEV - 1)]
        pltpu.make_async_copy(gone, gone, send_sem.at[turn_at]).wait()

    def put(turn_at, *rows):
        for at, row in enumerate(rows):
            send[turn_at][:, at, :] = row

    def y_forward(field):
        cos, sin = y_twist[0], y_twist[1]
        re_rows, im_rows = [[] for _ in range(SLOTS)], [[] for _ in range(SLOTS)]
        for comp in range(3):
            part = [field[comp][:, 512 * n : 512 * (n + 1)] for n in range(4)]
            even, odd = part[0] + part[2], part[1] + part[3]
            left, right = part[0] - part[2], part[1] - part[3]
            pairs = [(even + odd, None), (left, -right), (even - odd, None), (left, right), (even + odd, None)]
            for slot, (re, im) in enumerate(pairs):
                c, s = cos[slot : slot + 1], sin[slot : slot + 1]
                if slot == 0:
                    re_rows[slot].append(re)
                    im_rows[slot].append(jnp.zeros_like(re))
                elif im is None:
                    re_rows[slot].append(re * c)
                    im_rows[slot].append(-(re * s))
                else:
                    re_rows[slot].append(re * c + im * s)
                    im_rows[slot].append(im * c - re * s)
        pad = jnp.zeros((8, 512), F32)
        re = jnp.concatenate(sum(re_rows, []) + [pad], 0)
        im = jnp.concatenate(sum(im_rows, []) + [pad], 0)
        re_high, re_low = halves(re)
        im_high, im_low = halves(im)

        def arrange(r, i):
            return jnp.concatenate([jnp.concatenate([r, i], 1), jnp.concatenate([i, -r], 1)], 0)

        out = product(
            (y_table[0], y_table[1]), (arrange(re_high, im_high), arrange(re_low, im_low)), NT
        )
        return out[:, :128], out[:, 128:]

    def swap(value):
        even = lax.rem(lax.broadcasted_iota(jnp.int32, value.shape, 1), 2) == 0
        return jnp.where(even, pltpu.roll(value, 255, 1), pltpu.roll(value, 1, 1))

    def y_inverse(turn_at):
        re = recv[turn_at][:, 0, :].T
        im = recv[turn_at][:, 1, :].T
        if turn_at == 1:
            arrive(4)
            rest = recv[4][:, 0, :].T
            kept[0] = swap(jnp.concatenate([rest[0:64], re[120:128]], 0))
            kept[1] = swap(jnp.concatenate([rest[64:128], im[120:128]], 0))
        re = halves(jnp.concatenate([re[:24], re[24:96] + kept[0], re[96:]], 0))
        im = halves(jnp.concatenate([im[:24], im[24:96] + kept[1], im[96:]], 0))

        def arrange(r, i):
            return jnp.concatenate([jnp.concatenate([r, -i], 1), jnp.concatenate([i, r], 1)], 0)

        def tall(n):
            return jnp.concatenate([y_table[n, :, :512], y_table[n, :, 512:]], 0)

        out = product((arrange(re[0], im[0]), arrange(re[1], im[1])), (tall(0), tall(1)))
        cos, sin = y_twist[0], y_twist[1]

        def turned(slot, comp, want_im):
            a = out[lane(slot, comp, 0) : lane(slot, comp, 8)]
            if slot == 0:
                return a, None
            b = out[128 + lane(slot, comp, 0) : 128 + lane(slot, comp, 8)]
            c, s = cos[slot : slot + 1], sin[slot : slot + 1]
            return a * c - b * s, (b * c + a * s) if want_im else None

        field = []
        for comp in range(3):
            base = turned(0, comp, False)[0] + turned(4, comp, False)[0]
            one_re, one_im = turned(1, comp, True)
            two_re, _ = turned(2, comp, False)
            three_re, three_im = turned(3, comp, True)
            up, down = base + two_re, base - two_re
            re_sum, im_dif = one_re + three_re, one_im - three_im
            field.append([up + re_sum, down - im_dif, up - re_sum, down + im_dif])
        return field

    def x_transform(re, im, sign):
        re_high, re_low = halves(re)
        im_high, im_low = halves(im)

        def arrange(r, i):
            if sign < 0:
                return jnp.concatenate([jnp.concatenate([r, i], 1), jnp.concatenate([i, -r], 1)], 0)
            return jnp.concatenate([jnp.concatenate([r, i], 1), jnp.concatenate([-i, r], 1)], 0)

        out = product(
            (x_table[0], x_table[1]), (arrange(re_high, im_high), arrange(re_low, im_low))
        )
        return out[:, :128], out[:, 128:]

    def twist(re, im, sign):
        cos, sin = x_twist[0], x_twist[1]
        if sign < 0:
            return re * cos + im * sin, im * cos - re * sin
        return re * cos - im * sin, im * cos + re * sin

    def x_forward(turn_at):
        re, im = x_transform(recv[turn_at][:, 0, :], recv[turn_at][:, 1, :], -1)
        re, im = twist(re, im, -1)
        out = product(halves(jnp.concatenate([re, im], 1)), (eights[0, 0], eights[0, 1]))
        return out[:, :128], out[:, 128:]

    def x_inverse(re, im):
        out = product(halves(jnp.concatenate([re, im], 1)), (eights[1, 0], eights[1, 1]))
        re, im = twist(out[:, :128], out[:, 128:], 1)
        return x_transform(re, im, 1)

    for name in ("slip_rate", "y_twist", "y_table"):
        loads[name].wait()
    put(0, *y_forward([slip_rate[comp] for comp in range(3)]))

    def live(band, lag, comp):
        kept = (band_len[band] > lag).astype(F32)
        return kern[comp, band, lag] * kept

    effective = {
        (band, lag, comp): live(band, lag, comp)
        for lag in (0, 1, 2, 3) for comp in range(3) for band in range(BANDS)
    }
    effective.update({(0, lag, comp): live(0, lag, comp) for lag in range(4, LAGS) for comp in range(3)})

    for name in ("mode_band", "history", "past", "x_twist", "x_table"):
        loads[name].wait()

    def gather(mode, carry):
        at = pl.multiple_of(mode * 256, 256)
        band = mode_band[:, pl.ds(at, 256)]
        chosen = [band == b for b in range(BANDS)]
        for comp in range(3):
            total = [jnp.zeros((8, 256), F32), jnp.zeros((8, 256), F32)]
            for lag in range(2, LAGS):
                weight = jnp.zeros((8, 256), F32)
                for b in range(BANDS if lag < 4 else 1):
                    weight = jnp.where(chosen[b], effective[b, lag, comp], weight)
                for part in range(2):
                    source = history[lag - 2, comp, part, :, pl.ds(at, 256)].astype(F32)
                    total[part] = total[part] + weight * source
            for part in range(2):
                row = pl.multiple_of(((comp * 2 + part) * 8 + mode) * 8, 8)
                stacked[pl.ds(row, 8), :] = total[part]
        row = pl.multiple_of(mode * 8, 8)
        bands[pl.ds(row, 8), :] = band.astype(F32)
        return carry

    lax.fori_loop(0, 8, gather, 0)
    flat = halves(stacked[...].T)
    out = product(flat, (past[0], past[1]))
    sign = 1.0 - 2.0 * half.astype(F32)
    held_re, held_im = x_transform(*twist(out[:, :128], out[:, 128:256], 1), 1)
    hold[0] = held_re
    hold[1] = held_im * sign
    rest_re, rest_im = twist(out[:, 256:384], out[:, 384:], 1)
    rest_re, rest_im = halves(rest_re), halves(rest_im)
    rest = product(
        (x_table[0], x_table[1]),
        tuple(jnp.concatenate([rest_re[n], -rest_im[n]], 0) for n in range(2)),
    )
    lane_at = lax.broadcasted_iota(jnp.int32, (1, 128), 1)
    send_4[:, 0, :] = rest * jnp.where(lane_at < 64, 1.0, sign)

    pl.semaphore_wait(barrier, DEV - 1)
    band_copy = pltpu.make_async_remote_copy(
        mode_band.at[pl.ds(4, 4)], partner_band.at[pl.ds(4, 4)], pair_send.at[0], pair_recv.at[0],
        device_id=partner_id, device_id_type=MESH,
    )
    band_copy.start()
    exchange(0, True)
    exchange(4, False)
    for name in ("turn", "picks", "missing", "eights", "slip_field", "prestress"):
        loads[name].wait()

    band_copy.wait()
    for mode in range(8):
        bands[64 + mode * 8 : 72 + mode * 8, :] = partner_band[:, mode * 256 : (mode + 1) * 256].astype(F32)
    plain = bands[...].T.astype(BF16)
    dot = functools.partial(lax.dot_general, dimension_numbers=NN, preferred_element_type=F32)
    turned = dot(turn[...], plain).astype(BF16)
    first_row = lax.broadcasted_iota(jnp.int32, (256, 128), 0) == 0
    plain_band = dot(plain, picks[0]) + missing[0, 0:1]
    turned_band = (
        jnp.where(first_row, dot(turned, picks[2]), dot(turned, picks[1]))
        + missing[1, 0:1]
    )
    lane_comp = lax.rem(lane_at // 8, 3)
    weight = [jnp.zeros((256, 128), F32) for _ in range(2)]
    for which in (plain_band, turned_band):
        chosen = [jnp.zeros((256, 128), F32) for _ in range(2)]
        for b in range(BANDS):
            hit = which == float(b)
            for lag in range(2):
                value = jnp.where(
                    lane_comp == 0, effective[b, lag, 0],
                    jnp.where(lane_comp == 1, effective[b, lag, 1], effective[b, lag, 2]),
                )
                chosen[lag] = jnp.where(hit, value, chosen[lag])
        weight = [weight[lag] + chosen[lag] for lag in range(2)]
    first_weight = weight[0] + weight[1]
    now_weight = weight[1] + 0.5 * weight[0]
    tried_weight = 0.5 * weight[0]

    coeff = weakening(slip_field[0], slip_field[1])

    arrive(0)
    now_re, now_im = x_forward(0)
    re, im = x_inverse(now_re * first_weight, now_im * first_weight)
    put(1, re + hold[0], im + hold[1])
    exchange(1, False)
    re, im = x_inverse(now_re * now_weight, now_im * now_weight)
    hold[0] = re + hold[0]
    hold[1] = im + hold[1]
    arrive(1)
    field = y_inverse(1)
    stress = [prestress[comp] + jnp.concatenate(field[comp], 1) for comp in range(3)]

    put(2, *y_forward(slide(stress, coeff)))
    exchange(2, True)
    arrive(2)
    re, im = x_forward(2)
    re, im = x_inverse(re * tried_weight, im * tried_weight)
    put(3, re + hold[0], im + hold[1])
    exchange(3, False)
    arrive(3)
    field = y_inverse(3)
    for comp in range(3):
        for n in range(4):
            part = slice(512 * n, 512 * (n + 1))
            stress_out[comp, :, part] = prestress[comp, :, part] + field[comp][n]
    for turn_at in range(5):
        sent(turn_at)


def finish(stress, slip_field, slip_rate, new_rate, new_slip):
    coeff = weakening(slip_field[0], slip_field[1])
    for comp, value in enumerate(slide([stress[comp] for comp in range(3)], coeff)):
        new_rate[comp] = value
        new_slip[comp] = slip_field[comp] + 0.25 * (slip_rate[comp] + value)


def on_device(slip_rate, slip_field, prestress, history, kernel, band_len, mode_band):
    vmem = pl.BlockSpec(memory_space=pltpu.VMEM)
    smem = pl.BlockSpec(memory_space=pltpu.SMEM)
    anywhere = pl.BlockSpec(memory_space=pltpu.HBM)
    constants = [jnp.asarray(table) for table in tables()]
    halved = (5, 6, 7)
    shape = jax.ShapeDtypeStruct((3, 8, N), F32)
    dma = pltpu.SemaphoreType.DMA
    inputs = (slip_rate, slip_field, prestress, history, mode_band)
    stress = pl.pallas_call(
        body,
        out_shape=shape,
        in_specs=[anywhere] * (5 + len(constants)) + [smem] * 2,
        out_specs=vmem,
        scratch_shapes=[
            *[pltpu.VMEM(value.shape, value.dtype) for value in inputs],
            *[
                pltpu.VMEM(value.shape[1:] if at in halved else value.shape, value.dtype)
                for at, value in enumerate(constants)
            ],
            *[pltpu.VMEM((DEV, rows, 128), F32) for rows in (2, 2, 2, 2, 1) * 2],
            pltpu.VMEM((384, 256), F32),
            pltpu.VMEM((128, 256), F32),
            pltpu.VMEM((2, 256, 128), F32),
            pltpu.VMEM((2, 72, 256), F32),
            pltpu.VMEM((8, N), jnp.int32),
            dma((5,)), dma((5,)), dma((1,)), dma((1,)), dma((14,)),
        ],
        compiler_params=pltpu.CompilerParams(
            collective_id=0, has_side_effects=True, vmem_limit_bytes=67043328
        ),
    )(*inputs, *constants, jnp.transpose(kernel, (2, 0, 1)), band_len)
    return pl.pallas_call(
        finish, out_shape=(shape, shape), in_specs=[vmem] * 3, out_specs=(vmem, vmem)
    )(stress, slip_field, slip_rate)


def solution(mesh):
    rows = P(None, ("kx", "ky"), None)
    return jax.shard_map(
        on_device,
        mesh=mesh,
        in_specs=(
            rows, rows, rows, P(None, None, None, ("kx", "ky"), None), P(), P(), P(("kx", "ky"), None),
        ),
        out_specs=(rows, rows),
        check_vma=False,
    )
```

```python
import functools

import jax
import jax.numpy as jnp
import numpy as np
from jax import lax
from jax.experimental import pallas as pl
from jax.experimental.pallas import tpu as pltpu
from jax.sharding import PartitionSpec as P

MESH = pl.DeviceIdType.MESH
N = 2048
DEV = 256
SLOTS = 5
BANDS = 8
LAGS = 8
F32 = jnp.float32
BF16 = jnp.bfloat16


def split(table):
    table = np.asarray(table, np.float64)
    high = table.astype(np.float32).astype(jnp.bfloat16)
    low = (table - high.astype(np.float64)).astype(np.float32).astype(jnp.bfloat16)
    return np.stack([np.asarray(high), np.asarray(low)])


def lane(slot, comp, at):
    return slot * 24 + comp * 8 + at


@functools.cache
def tables():
    scale = 1.0 / np.sqrt(N)
    k2, n2 = np.arange(256)[:, None], np.arange(512)[None, :]
    angle = 2 * np.pi / 512 * (k2 * n2 % 512)
    y_table = split(np.concatenate([np.cos(angle), np.sin(angle)], 1) * scale)
    k1, s = np.arange(256)[:, None], np.arange(256)[None, :]
    angle = 2 * np.pi / 256 * (k1 * s % 256)
    x_table = split(np.concatenate([np.cos(angle), np.sin(angle)], 1) * scale)
    slots = np.arange(8)[:, None]
    angle = 2 * np.pi / N * (slots * n2 % N)
    y_twist = np.stack([np.cos(angle), np.sin(angle)]).astype(np.float32)
    x_twist = np.zeros((2, 256, 128), np.float32)
    eight = np.arange(8)
    for group in range(16):
        angle = 2 * np.pi / N * (np.arange(256)[:, None] * eight[None, :])
        x_twist[0, :, group * 8 : group * 8 + 8] = np.cos(angle)
        x_twist[1, :, group * 8 : group * 8 + 8] = np.sin(angle)
    angle = 2 * np.pi / 8 * (eight[:, None] * eight[None, :] % 8)
    cos8, sin8 = np.cos(angle), np.sin(angle)
    forward = np.zeros((256, 256))
    inverse = np.zeros((256, 256))
    for slot in range(SLOTS):
        for comp in range(3):
            at = lane(slot, comp, 0)
            re, im = slice(at, at + 8), slice(128 + at, 128 + at + 8)
            forward[re, re], forward[im, re] = cos8, sin8
            forward[re, im], forward[im, im] = -sin8, cos8
            inverse[re, re], inverse[im, re] = cos8, -sin8
            inverse[re, im], inverse[im, im] = sin8, cos8
    eights = np.stack([split(forward), split(inverse)])
    past = np.zeros((2, 384, 512))

    def fill(table, out_re, out_im, comp, row, turned):
        re, im = slice(out_re, out_re + 8), slice(out_im, out_im + 8)
        for mode in range(8):
            in_re = ((comp * 2 + 0) * 8 + mode) * 8 + row
            in_im = ((comp * 2 + 1) * 8 + mode) * 8 + row
            if turned:
                table[in_re, re], table[in_im, re] = sin8[mode], cos8[mode]
                table[in_re, im], table[in_im, im] = -cos8[mode], sin8[mode]
            else:
                table[in_re, re], table[in_im, re] = cos8[mode], -sin8[mode]
                table[in_re, im], table[in_im, im] = sin8[mode], cos8[mode]

    for half, (own, other) in enumerate((((0, 1, 2, 3, 4), (5, 6, 7)), ((4, 3, 2, 1, 0), (7, 6, 5)))):
        for slot, row in enumerate(own):
            for comp in range(3):
                at = lane(slot, comp, 0)
                fill(past[half], at, 128 + at, comp, row, False)
        for slot, row in enumerate(other):
            for comp in range(3):
                group = slot * 3 + comp
                if group == 8:
                    fill(past[half], 120, 248, comp, row, False)
                else:
                    at = 256 + group * 8
                    fill(past[half], at, 128 + at, comp, row, False)
                    fill(past[half], at + 64, 192 + at, comp, row, True)
    past = np.stack([split(past[0]), split(past[1])])
    picks = np.zeros((2, 3, 128, 128), np.float32)
    missing = np.full((2, 2, 8, 128), 8.0, np.float32)
    plain = [{slot: (0, slot) for slot in range(4)}, {slot: (1, 4 + slot) for slot in range(4)}]
    turned = [{slot: (1, 8 - slot) for slot in (1, 2, 3)}, {slot: (0, 4 - slot) for slot in range(5)}]
    for half in range(2):
        for kind, (which, source) in enumerate(
            ((plain, eight), (turned, 7 - eight), (turned, (8 - eight) % 8))
        ):
            for slot, (block, row) in which[half].items():
                for comp in range(3):
                    for mode in range(8):
                        out = lane(slot, comp, mode)
                        picks[half, kind, (block * 8 + source[mode]) * 8 + row, out] = 1.0
                        missing[half, min(kind, 1), :, out] = 0.0
    picks = picks.astype(jnp.bfloat16)
    turn = np.zeros((256, 256), np.float32)
    turn[np.arange(256), (256 - np.arange(256)) % 256] = 1.0
    turn = turn.astype(jnp.bfloat16)
    return y_table, x_table, y_twist, x_twist, eights, past, picks, missing, turn


def halves(value):
    high = value.astype(BF16)
    low = (value - high.astype(F32)).astype(BF16)
    return high, low


NN = (((1,), (0,)), ((), ()))
NT = (((1,), (1,)), ((), ()))


def product(left, right, dims=NN):
    (left_high, left_low), (right_high, right_low) = left, right
    dot = functools.partial(lax.dot_general, dimension_numbers=dims, preferred_element_type=F32)
    return dot(left_high, right_high) + (dot(left_high, right_low) + dot(left_low, right_high))


def softplus(value):
    return jnp.maximum(value, 0.0) + jnp.log1p(jnp.exp(-jnp.abs(value)))


def block_of(device):
    return 2 * device + lax.div(device, 128) * (511 - 4 * device)


def slide(stress, coeff):
    strength = coeff * softplus(-stress[2])
    magnitude = jnp.sqrt(stress[0] * stress[0] + stress[1] * stress[1] + 1.0)
    ratio = softplus(magnitude - strength) / magnitude
    return ratio * stress[0], ratio * stress[1], softplus(stress[2])


def weakening(first, second):
    worn = jnp.sqrt(first * first + second * second + 1.0) - 1.0
    return 0.35 + 0.35 * jnp.exp(worn * -2.0)


def body(
    slip_rate_in, slip_field_in, prestress_in, history_in, mode_band_in,
    y_table_in, x_table_in, y_twist_in, x_twist_in, eights_in, past_in, picks_in, missing_in, turn_in,
    kern, band_len,
    stress_out,
    slip_rate, slip_field, prestress, history, mode_band,
    y_table, x_table, y_twist, x_twist, eights, past, picks, missing, turn,
    send_0, send_1, send_2, send_3, send_4, recv_0, recv_1, recv_2, recv_3, recv_4,
    stacked, bands, hold, kept, partner_band,
    send_sem, recv_sem, pair_send, pair_recv, load_sem,
):
    kx, ky = lax.axis_index("kx"), lax.axis_index("ky")
    me = kx * 8 + ky
    half = me // 128
    mine = block_of(me)
    partner = 255 - me
    partner_id = (partner // 8, lax.rem(partner, 8))
    send = (send_0, send_1, send_2, send_3, send_4)
    recv = (recv_0, recv_1, recv_2, recv_3, recv_4)

    barrier = pltpu.get_barrier_semaphore()

    def greet(other):
        pl.semaphore_signal(
            barrier, inc=1, device_id=(lax.div(other, 8), lax.rem(other, 8)), device_id_type=MESH
        )

    def greet_two(step, carry):
        greet(lax.rem(me + 128 + step, DEV))
        greet(lax.rem(me + 128 - step, DEV))
        return carry

    greet(lax.rem(me + 128, DEV))
    greet(lax.rem(me + 129, DEV))
    greet(lax.rem(me + 127, DEV))
    lax.fori_loop(2, 128, greet_two, 0, unroll=7)

    partner_band[0:4] = jnp.zeros((4, N), jnp.int32)
    loads = {}
    for at, (name, source, target) in enumerate((
        ("slip_rate", slip_rate_in, slip_rate),
        ("y_twist", y_twist_in, y_twist),
        ("y_table", y_table_in, y_table),
        ("mode_band", mode_band_in, mode_band),
        ("history", history_in, history),
        ("past", past_in.at[half], past),
        ("x_twist", x_twist_in, x_twist),
        ("x_table", x_table_in, x_table),
        ("turn", turn_in, turn),
        ("picks", picks_in.at[half], picks),
        ("missing", missing_in.at[half], missing),
        ("eights", eights_in, eights),
        ("slip_field", slip_field_in, slip_field),
        ("prestress", prestress_in, prestress),
    )):
        loads[name] = pltpu.make_async_copy(source, target, load_sem.at[at])
        loads[name].start()

    def exchange(turn_at, forward):
        def one(device):
            if forward:
                source, target = send[turn_at].at[block_of(device)], recv[turn_at].at[me]
            else:
                source, target = send[turn_at].at[device], recv[turn_at].at[mine]
            pltpu.make_async_remote_copy(
                source, target, send_sem.at[turn_at], recv_sem.at[turn_at],
                device_id=(lax.div(device, 8), lax.rem(device, 8)), device_id_type=MESH,
            ).start()

        one(lax.rem(me + 128, DEV))
        one(lax.rem(me + 129, DEV))
        one(lax.rem(me + 127, DEV))

        def two(step, carry):
            one(lax.rem(me + 128 + step, DEV))
            one(lax.rem(me + 128 - step, DEV))
            return carry

        lax.fori_loop(2, 128, two, 0, unroll=7)
        if forward:
            source, target = send[turn_at].at[mine], recv[turn_at].at[me]
        else:
            source, target = send[turn_at].at[me], recv[turn_at].at[mine]
        pltpu.make_async_copy(source, target, recv_sem.at[turn_at]).start()

    def arrive(turn_at):
        whole = recv[turn_at]
        pltpu.make_async_copy(whole, whole, recv_sem.at[turn_at]).wait()

    def sent(turn_at):
        gone = send[turn_at].at[pl.ds(0, DEV - 1)]
        pltpu.make_async_copy(gone, gone, send_sem.at[turn_at]).wait()

    def put(turn_at, *rows):
        for at, row in enumerate(rows):
            send[turn_at][:, at, :] = row

    def y_forward(field):
        cos, sin = y_twist[0], y_twist[1]
        re_rows, im_rows = [[] for _ in range(SLOTS)], [[] for _ in range(SLOTS)]
        for comp in range(3):
            part = [field[comp][:, 512 * n : 512 * (n + 1)] for n in range(4)]
            even, odd = part[0] + part[2], part[1] + part[3]
            left, right = part[0] - part[2], part[1] - part[3]
            pairs = [(even + odd, None), (left, -right), (even - odd, None), (left, right), (even + odd, None)]
            for slot, (re, im) in enumerate(pairs):
                c, s = cos[slot : slot + 1], sin[slot : slot + 1]
                if slot == 0:
                    re_rows[slot].append(re)
                    im_rows[slot].append(jnp.zeros_like(re))
                elif im is None:
                    re_rows[slot].append(re * c)
                    im_rows[slot].append(-(re * s))
                else:
                    re_rows[slot].append(re * c + im * s)
                    im_rows[slot].append(im * c - re * s)
        pad = jnp.zeros((8, 512), F32)
        re = jnp.concatenate(sum(re_rows, []) + [pad], 0)
        im = jnp.concatenate(sum(im_rows, []) + [pad], 0)
        re_high, re_low = halves(re)
        im_high, im_low = halves(im)

        def arrange(r, i):
            return jnp.concatenate([jnp.concatenate([r, i], 1), jnp.concatenate([i, -r], 1)], 0)

        out = product(
            (y_table[0], y_table[1]), (arrange(re_high, im_high), arrange(re_low, im_low)), NT
        )
        return out[:, :128], out[:, 128:]

    def swap(value):
        even = lax.rem(lax.broadcasted_iota(jnp.int32, value.shape, 1), 2) == 0
        return jnp.where(even, pltpu.roll(value, 255, 1), pltpu.roll(value, 1, 1))

    def y_inverse(turn_at):
        re = recv[turn_at][:, 0, :].T
        im = recv[turn_at][:, 1, :].T
        if turn_at == 1:
            arrive(4)
            rest = recv[4][:, 0, :].T
            kept[0] = swap(jnp.concatenate([rest[0:64], re[120:128]], 0))
            kept[1] = swap(jnp.concatenate([rest[64:128], im[120:128]], 0))
        re = halves(jnp.concatenate([re[:24], re[24:96] + kept[0], re[96:]], 0))
        im = halves(jnp.concatenate([im[:24], im[24:96] + kept[1], im[96:]], 0))

        def arrange(r, i):
            return jnp.concatenate([jnp.concatenate([r, -i], 1), jnp.concatenate([i, r], 1)], 0)

        def tall(n):
            return jnp.concatenate([y_table[n, :, :512], y_table[n, :, 512:]], 0)

        out = product((arrange(re[0], im[0]), arrange(re[1], im[1])), (tall(0), tall(1)))
        cos, sin = y_twist[0], y_twist[1]

        def turned(slot, comp, want_im):
            a = out[lane(slot, comp, 0) : lane(slot, comp, 8)]
            if slot == 0:
                return a, None
            b = out[128 + lane(slot, comp, 0) : 128 + lane(slot, comp, 8)]
            c, s = cos[slot : slot + 1], sin[slot : slot + 1]
            return a * c - b * s, (b * c + a * s) if want_im else None

        field = []
        for comp in range(3):
            base = turned(0, comp, False)[0] + turned(4, comp, False)[0]
            one_re, one_im = turned(1, comp, True)
            two_re, _ = turned(2, comp, False)
            three_re, three_im = turned(3, comp, True)
            up, down = base + two_re, base - two_re
            re_sum, im_dif = one_re + three_re, one_im - three_im
            field.append([up + re_sum, down - im_dif, up - re_sum, down + im_dif])
        return field

    def x_transform(re, im, sign):
        re_high, re_low = halves(re)
        im_high, im_low = halves(im)

        def arrange(r, i):
            if sign < 0:
                return jnp.concatenate([jnp.concatenate([r, i], 1), jnp.concatenate([i, -r], 1)], 0)
            return jnp.concatenate([jnp.concatenate([r, i], 1), jnp.concatenate([-i, r], 1)], 0)

        out = product(
            (x_table[0], x_table[1]), (arrange(re_high, im_high), arrange(re_low, im_low))
        )
        return out[:, :128], out[:, 128:]

    def twist(re, im, sign):
        cos, sin = x_twist[0], x_twist[1]
        if sign < 0:
            return re * cos + im * sin, im * cos - re * sin
        return re * cos - im * sin, im * cos + re * sin

    def x_forward(turn_at):
        re, im = x_transform(recv[turn_at][:, 0, :], recv[turn_at][:, 1, :], -1)
        re, im = twist(re, im, -1)
        out = product(halves(jnp.concatenate([re, im], 1)), (eights[0, 0], eights[0, 1]))
        return out[:, :128], out[:, 128:]

    def x_inverse(re, im):
        out = product(halves(jnp.concatenate([re, im], 1)), (eights[1, 0], eights[1, 1]))
        re, im = twist(out[:, :128], out[:, 128:], 1)
        return x_transform(re, im, 1)

    for name in ("slip_rate", "y_twist", "y_table"):
        loads[name].wait()
    put(0, *y_forward([slip_rate[comp] for comp in range(3)]))

    def live(band, lag, comp):
        kept = (band_len[band] > lag).astype(F32)
        return kern[comp, band, lag] * kept

    effective = {
        (band, lag, comp): live(band, lag, comp)
        for lag in (0, 1, 2, 3) for comp in range(3) for band in range(BANDS)
    }
    effective.update({(0, lag, comp): live(0, lag, comp) for lag in range(4, LAGS) for comp in range(3)})

    for name in ("mode_band", "history", "past", "x_twist", "x_table"):
        loads[name].wait()

    def gather(mode, carry):
        at = pl.multiple_of(mode * 256, 256)
        band = mode_band[:, pl.ds(at, 256)]
        chosen = [band == b for b in range(BANDS)]
        for comp in range(3):
            total = [jnp.zeros((8, 256), F32), jnp.zeros((8, 256), F32)]
            for lag in range(2, LAGS):
                weight = jnp.zeros((8, 256), F32)
                for b in range(BANDS if lag < 4 else 1):
                    weight = jnp.where(chosen[b], effective[b, lag, comp], weight)
                for part in range(2):
                    source = history[lag - 2, comp, part, :, pl.ds(at, 256)].astype(F32)
                    total[part] = total[part] + weight * source
            for part in range(2):
                row = pl.multiple_of(((comp * 2 + part) * 8 + mode) * 8, 8)
                stacked[pl.ds(row, 8), :] = total[part]
        row = pl.multiple_of(mode * 8, 8)
        bands[pl.ds(row, 8), :] = band.astype(F32)
        return carry

    lax.fori_loop(0, 8, gather, 0)
    flat = halves(stacked[...].T)
    out = product(flat, (past[0], past[1]))
    sign = 1.0 - 2.0 * half.astype(F32)
    held_re, held_im = x_transform(*twist(out[:, :128], out[:, 128:256], 1), 1)
    hold[0] = held_re
    hold[1] = held_im * sign
    rest_re, rest_im = twist(out[:, 256:384], out[:, 384:], 1)
    rest_re, rest_im = halves(rest_re), halves(rest_im)
    rest = product(
        (x_table[0], x_table[1]),
        tuple(jnp.concatenate([rest_re[n], -rest_im[n]], 0) for n in range(2)),
    )
    lane_at = lax.broadcasted_iota(jnp.int32, (1, 128), 1)
    send_4[:, 0, :] = rest * jnp.where(lane_at < 64, 1.0, sign)

    pl.semaphore_wait(barrier, DEV - 1)
    band_copy = pltpu.make_async_remote_copy(
        mode_band.at[pl.ds(4, 4)], partner_band.at[pl.ds(4, 4)], pair_send.at[0], pair_recv.at[0],
        device_id=partner_id, device_id_type=MESH,
    )
    band_copy.start()
    exchange(0, True)
    exchange(4, False)
    for name in ("turn", "picks", "missing", "eights", "slip_field", "prestress"):
        loads[name].wait()

    band_copy.wait()
    for mode in range(8):
        bands[64 + mode * 8 : 72 + mode * 8, :] = partner_band[:, mode * 256 : (mode + 1) * 256].astype(F32)
    plain = bands[...].T.astype(BF16)
    dot = functools.partial(lax.dot_general, dimension_numbers=NN, preferred_element_type=F32)
    turned = dot(turn[...], plain).astype(BF16)
    first_row = lax.broadcasted_iota(jnp.int32, (256, 128), 0) == 0
    plain_band = dot(plain, picks[0]) + missing[0, 0:1]
    turned_band = (
        jnp.where(first_row, dot(turned, picks[2]), dot(turned, picks[1]))
        + missing[1, 0:1]
    )
    lane_comp = lax.rem(lane_at // 8, 3)
    weight = [jnp.zeros((256, 128), F32) for _ in range(2)]
    for which in (plain_band, turned_band):
        chosen = [jnp.zeros((256, 128), F32) for _ in range(2)]
        for b in range(BANDS):
            hit = which == float(b)
            for lag in range(2):
                value = jnp.where(
                    lane_comp == 0, effective[b, lag, 0],
                    jnp.where(lane_comp == 1, effective[b, lag, 1], effective[b, lag, 2]),
                )
                chosen[lag] = jnp.where(hit, value, chosen[lag])
        weight = [weight[lag] + chosen[lag] for lag in range(2)]
    first_weight = weight[0] + weight[1]
    now_weight = weight[1] + 0.5 * weight[0]
    tried_weight = 0.5 * weight[0]

    coeff = weakening(slip_field[0], slip_field[1])

    arrive(0)
    now_re, now_im = x_forward(0)
    re, im = x_inverse(now_re * first_weight, now_im * first_weight)
    put(1, re + hold[0], im + hold[1])
    exchange(1, False)
    re, im = x_inverse(now_re * now_weight, now_im * now_weight)
    hold[0] = re + hold[0]
    hold[1] = im + hold[1]
    arrive(1)
    field = y_inverse(1)
    stress = [prestress[comp] + jnp.concatenate(field[comp], 1) for comp in range(3)]

    put(2, *y_forward(slide(stress, coeff)))
    exchange(2, True)
    arrive(2)
    re, im = x_forward(2)
    re, im = x_inverse(re * tried_weight, im * tried_weight)
    put(3, re + hold[0], im + hold[1])
    exchange(3, False)
    arrive(3)
    field = y_inverse(3)
    for comp in range(3):
        for n in range(4):
            part = slice(512 * n, 512 * (n + 1))
            stress_out[comp, :, part] = prestress[comp, :, part] + field[comp][n]
    for turn_at in range(5):
        sent(turn_at)


def finish(stress, slip_field, slip_rate, new_rate, new_slip):
    coeff = weakening(slip_field[0], slip_field[1])
    for comp, value in enumerate(slide([stress[comp] for comp in range(3)], coeff)):
        new_rate[comp] = value
        new_slip[comp] = slip_field[comp] + 0.25 * (slip_rate[comp] + value)


def on_device(slip_rate, slip_field, prestress, history, kernel, band_len, mode_band):
    vmem = pl.BlockSpec(memory_space=pltpu.VMEM)
    smem = pl.BlockSpec(memory_space=pltpu.SMEM)
    anywhere = pl.BlockSpec(memory_space=pltpu.HBM)
    constants = [jnp.asarray(table) for table in tables()]
    halved = (5, 6, 7)
    shape = jax.ShapeDtypeStruct((3, 8, N), F32)
    dma = pltpu.SemaphoreType.DMA
    inputs = (slip_rate, slip_field, prestress, history, mode_band)
    stress = pl.pallas_call(
        body,
        out_shape=shape,
        in_specs=[anywhere] * (5 + len(constants)) + [smem] * 2,
        out_specs=vmem,
        scratch_shapes=[
            *[pltpu.VMEM(value.shape, value.dtype) for value in inputs],
            *[
                pltpu.VMEM(value.shape[1:] if at in halved else value.shape, value.dtype)
                for at, value in enumerate(constants)
            ],
            *[pltpu.VMEM((DEV, rows, 128), F32) for rows in (2, 2, 2, 2, 1) * 2],
            pltpu.VMEM((384, 256), F32),
            pltpu.VMEM((128, 256), F32),
            pltpu.VMEM((2, 256, 128), F32),
            pltpu.VMEM((2, 72, 256), F32),
            pltpu.VMEM((8, N), jnp.int32),
            dma((5,)), dma((5,)), dma((1,)), dma((1,)), dma((14,)),
        ],
        compiler_params=pltpu.CompilerParams(
            collective_id=0, has_side_effects=True, vmem_limit_bytes=62 * 1024 * 1024
        ),
    )(*inputs, *constants, jnp.transpose(kernel, (2, 0, 1)), band_len)
    return pl.pallas_call(
        finish, out_shape=(shape, shape), in_specs=[vmem] * 3, out_specs=(vmem, vmem),
        compiler_params=pltpu.CompilerParams(vmem_limit_bytes=4 * 1024 * 1024),
    )(stress, slip_field, slip_rate)


def solution(mesh):
    rows = P(None, ("kx", "ky"), None)
    return jax.shard_map(
        on_device,
        mesh=mesh,
        in_specs=(
            rows, rows, rows, P(None, None, None, ("kx", "ky"), None), P(), P(), P(("kx", "ky"), None),
        ),
        out_specs=(rows, rows),
        check_vma=False,
    )
```

```python
import functools

import jax
import jax.numpy as jnp
import numpy as np
from jax import lax
from jax.experimental import pallas as pl
from jax.experimental.pallas import tpu as pltpu
from jax.sharding import PartitionSpec as P

MESH = pl.DeviceIdType.MESH
N = 2048
DEV = 256
SLOTS = 5
BANDS = 8
LAGS = 8
F32 = jnp.float32
BF16 = jnp.bfloat16


def split(table):
    table = np.asarray(table, np.float64)
    high = table.astype(np.float32).astype(jnp.bfloat16)
    low = (table - high.astype(np.float64)).astype(np.float32).astype(jnp.bfloat16)
    return np.stack([np.asarray(high), np.asarray(low)])


def lane(slot, comp, at):
    return slot * 24 + comp * 8 + at


@functools.cache
def tables():
    scale = 1.0 / np.sqrt(N)
    k2, n2 = np.arange(256)[:, None], np.arange(512)[None, :]
    angle = 2 * np.pi / 512 * (k2 * n2 % 512)
    y_table = split(np.concatenate([np.cos(angle), np.sin(angle)], 1) * scale)
    k1, s = np.arange(256)[:, None], np.arange(256)[None, :]
    angle = 2 * np.pi / 256 * (k1 * s % 256)
    x_table = split(np.concatenate([np.cos(angle), np.sin(angle)], 1) * scale)
    slots = np.arange(8)[:, None]
    angle = 2 * np.pi / N * (slots * n2 % N)
    y_twist = np.stack([np.cos(angle), np.sin(angle)]).astype(np.float32)
    x_twist = np.zeros((2, 256, 128), np.float32)
    eight = np.arange(8)
    for group in range(16):
        angle = 2 * np.pi / N * (np.arange(256)[:, None] * eight[None, :])
        x_twist[0, :, group * 8 : group * 8 + 8] = np.cos(angle)
        x_twist[1, :, group * 8 : group * 8 + 8] = np.sin(angle)
    angle = 2 * np.pi / 8 * (eight[:, None] * eight[None, :] % 8)
    cos8, sin8 = np.cos(angle), np.sin(angle)
    forward = np.zeros((256, 256))
    inverse = np.zeros((256, 256))
    for slot in range(SLOTS):
        for comp in range(3):
            at = lane(slot, comp, 0)
            re, im = slice(at, at + 8), slice(128 + at, 128 + at + 8)
            forward[re, re], forward[im, re] = cos8, sin8
            forward[re, im], forward[im, im] = -sin8, cos8
            inverse[re, re], inverse[im, re] = cos8, -sin8
            inverse[re, im], inverse[im, im] = sin8, cos8
    eights = np.stack([split(forward), split(inverse)])
    past = np.zeros((2, 384, 512))

    def fill(table, out_re, out_im, comp, row, turned):
        re, im = slice(out_re, out_re + 8), slice(out_im, out_im + 8)
        for mode in range(8):
            in_re = ((comp * 2 + 0) * 8 + mode) * 8 + row
            in_im = ((comp * 2 + 1) * 8 + mode) * 8 + row
            if turned:
                table[in_re, re], table[in_im, re] = sin8[mode], cos8[mode]
                table[in_re, im], table[in_im, im] = -cos8[mode], sin8[mode]
            else:
                table[in_re, re], table[in_im, re] = cos8[mode], -sin8[mode]
                table[in_re, im], table[in_im, im] = sin8[mode], cos8[mode]

    for half, (own, other) in enumerate((((0, 1, 2, 3, 4), (5, 6, 7)), ((4, 3, 2, 1, 0), (7, 6, 5)))):
        for slot, row in enumerate(own):
            for comp in range(3):
                at = lane(slot, comp, 0)
                fill(past[half], at, 128 + at, comp, row, False)
        for slot, row in enumerate(other):
            for comp in range(3):
                group = slot * 3 + comp
                if group == 8:
                    fill(past[half], 120, 248, comp, row, False)
                else:
                    at = 256 + group * 8
                    fill(past[half], at, 128 + at, comp, row, False)
                    fill(past[half], at + 64, 192 + at, comp, row, True)
    past = np.stack([split(past[0]), split(past[1])])
    picks = np.zeros((2, 3, 128, 128), np.float32)
    missing = np.full((2, 2, 8, 128), 8.0, np.float32)
    plain = [{slot: (0, slot) for slot in range(4)}, {slot: (1, 4 + slot) for slot in range(4)}]
    turned = [{slot: (1, 8 - slot) for slot in (1, 2, 3)}, {slot: (0, 4 - slot) for slot in range(5)}]
    for half in range(2):
        for kind, (which, source) in enumerate(
            ((plain, eight), (turned, 7 - eight), (turned, (8 - eight) % 8))
        ):
            for slot, (block, row) in which[half].items():
                for comp in range(3):
                    for mode in range(8):
                        out = lane(slot, comp, mode)
                        picks[half, kind, (block * 8 + source[mode]) * 8 + row, out] = 1.0
                        missing[half, min(kind, 1), :, out] = 0.0
    picks = picks.astype(jnp.bfloat16)
    turn = np.zeros((256, 256), np.float32)
    turn[np.arange(256), (256 - np.arange(256)) % 256] = 1.0
    turn = turn.astype(jnp.bfloat16)
    return y_table, x_table, y_twist, x_twist, eights, past, picks, missing, turn


def halves(value):
    high = value.astype(BF16)
    low = (value - high.astype(F32)).astype(BF16)
    return high, low


NN = (((1,), (0,)), ((), ()))
NT = (((1,), (1,)), ((), ()))


def product(left, right, dims=NN):
    (left_high, left_low), (right_high, right_low) = left, right
    dot = functools.partial(lax.dot_general, dimension_numbers=dims, preferred_element_type=F32)
    return dot(left_high, right_high) + (dot(left_high, right_low) + dot(left_low, right_high))


def softplus(value):
    return jnp.maximum(value, 0.0) + jnp.log1p(jnp.exp(-jnp.abs(value)))


def block_of(device):
    return 2 * device + lax.div(device, 128) * (511 - 4 * device)


def slide(stress, coeff):
    strength = coeff * softplus(-stress[2])
    magnitude = jnp.sqrt(stress[0] * stress[0] + stress[1] * stress[1] + 1.0)
    ratio = softplus(magnitude - strength) / magnitude
    return ratio * stress[0], ratio * stress[1], softplus(stress[2])


def weakening(first, second):
    worn = jnp.sqrt(first * first + second * second + 1.0) - 1.0
    return 0.35 + 0.35 * jnp.exp(worn * -2.0)


def body(
    slip_rate_in, slip_field_in, prestress_in, history_in, mode_band_in,
    y_table_in, x_table_in, y_twist_in, x_twist_in, eights_in, past_in, picks_in, missing_in, turn_in,
    kern, band_len,
    stress_out,
    slip_rate, slip_field, prestress, history, mode_band,
    y_table, x_table, y_twist, x_twist, eights, past, picks, missing, turn,
    send_0, send_1, send_2, send_3, send_4, recv_0, recv_1, recv_2, recv_3, recv_4,
    stacked, bands, hold, kept, partner_band,
    send_sem, recv_sem, pair_send, pair_recv, load_sem,
):
    kx, ky = lax.axis_index("kx"), lax.axis_index("ky")
    me = kx * 8 + ky
    half = me // 128
    mine = block_of(me)
    partner = 255 - me
    partner_id = (partner // 8, lax.rem(partner, 8))
    send = (send_0, send_1, send_2, send_3, send_4)
    recv = (recv_0, recv_1, recv_2, recv_3, recv_4)

    barrier = pltpu.get_barrier_semaphore()

    def greet(other):
        pl.semaphore_signal(
            barrier, inc=1, device_id=(lax.div(other, 8), lax.rem(other, 8)), device_id_type=MESH
        )

    def greet_two(step, carry):
        greet(lax.rem(me + 128 + step, DEV))
        greet(lax.rem(me + 128 - step, DEV))
        return carry

    greet(lax.rem(me + 128, DEV))
    greet(lax.rem(me + 129, DEV))
    greet(lax.rem(me + 127, DEV))
    lax.fori_loop(2, 128, greet_two, 0, unroll=7)

    partner_band[0:4] = jnp.zeros((4, N), jnp.int32)
    loads = {}
    for at, (name, source, target) in enumerate((
        ("slip_rate", slip_rate_in, slip_rate),
        ("y_twist", y_twist_in, y_twist),
        ("y_table", y_table_in, y_table),
        ("mode_band", mode_band_in, mode_band),
        ("history", history_in, history),
        ("past", past_in.at[half], past),
        ("x_twist", x_twist_in, x_twist),
        ("x_table", x_table_in, x_table),
        ("turn", turn_in, turn),
        ("picks", picks_in.at[half], picks),
        ("missing", missing_in.at[half], missing),
        ("eights", eights_in, eights),
        ("slip_field", slip_field_in, slip_field),
        ("prestress", prestress_in, prestress),
    )):
        loads[name] = pltpu.make_async_copy(source, target, load_sem.at[at])
        loads[name].start()

    def exchange(turn_at, forward):
        def one(device):
            if forward:
                source, target = send[turn_at].at[block_of(device)], recv[turn_at].at[me]
            else:
                source, target = send[turn_at].at[device], recv[turn_at].at[mine]
            pltpu.make_async_remote_copy(
                source, target, send_sem.at[turn_at], recv_sem.at[turn_at],
                device_id=(lax.div(device, 8), lax.rem(device, 8)), device_id_type=MESH,
            ).start()

        one(lax.rem(me + 128, DEV))
        one(lax.rem(me + 129, DEV))
        one(lax.rem(me + 127, DEV))

        def two(step, carry):
            one(lax.rem(me + 128 + step, DEV))
            one(lax.rem(me + 128 - step, DEV))
            return carry

        lax.fori_loop(2, 128, two, 0, unroll=14)
        if forward:
            source, target = send[turn_at].at[mine], recv[turn_at].at[me]
        else:
            source, target = send[turn_at].at[me], recv[turn_at].at[mine]
        pltpu.make_async_copy(source, target, recv_sem.at[turn_at]).start()

    def arrive(turn_at):
        whole = recv[turn_at]
        pltpu.make_async_copy(whole, whole, recv_sem.at[turn_at]).wait()

    def sent(turn_at):
        gone = send[turn_at].at[pl.ds(0, DEV - 1)]
        pltpu.make_async_copy(gone, gone, send_sem.at[turn_at]).wait()

    def put(turn_at, *rows):
        for at, row in enumerate(rows):
            send[turn_at][:, at, :] = row

    def y_forward(field):
        cos, sin = y_twist[0], y_twist[1]
        re_rows, im_rows = [[] for _ in range(SLOTS)], [[] for _ in range(SLOTS)]
        for comp in range(3):
            part = [field[comp][:, 512 * n : 512 * (n + 1)] for n in range(4)]
            even, odd = part[0] + part[2], part[1] + part[3]
            left, right = part[0] - part[2], part[1] - part[3]
            pairs = [(even + odd, None), (left, -right), (even - odd, None), (left, right), (even + odd, None)]
            for slot, (re, im) in enumerate(pairs):
                c, s = cos[slot : slot + 1], sin[slot : slot + 1]
                if slot == 0:
                    re_rows[slot].append(re)
                    im_rows[slot].append(jnp.zeros_like(re))
                elif im is None:
                    re_rows[slot].append(re * c)
                    im_rows[slot].append(-(re * s))
                else:
                    re_rows[slot].append(re * c + im * s)
                    im_rows[slot].append(im * c - re * s)
        pad = jnp.zeros((8, 512), F32)
        re = jnp.concatenate(sum(re_rows, []) + [pad], 0)
        im = jnp.concatenate(sum(im_rows, []) + [pad], 0)
        re_high, re_low = halves(re)
        im_high, im_low = halves(im)

        def arrange(r, i):
            return jnp.concatenate([jnp.concatenate([r, i], 1), jnp.concatenate([i, -r], 1)], 0)

        out = product(
            (y_table[0], y_table[1]), (arrange(re_high, im_high), arrange(re_low, im_low)), NT
        )
        return out[:, :128], out[:, 128:]

    def swap(value):
        even = lax.rem(lax.broadcasted_iota(jnp.int32, value.shape, 1), 2) == 0
        return jnp.where(even, pltpu.roll(value, 255, 1), pltpu.roll(value, 1, 1))

    def y_inverse(turn_at):
        re = recv[turn_at][:, 0, :].T
        im = recv[turn_at][:, 1, :].T
        if turn_at == 1:
            kept[0, 64:72] = swap(re[120:128])
            kept[1, 64:72] = swap(im[120:128])
        re = halves(jnp.concatenate([re[:24], re[24:96] + kept[0], re[96:]], 0))
        im = halves(jnp.concatenate([im[:24], im[24:96] + kept[1], im[96:]], 0))

        def arrange(r, i):
            return jnp.concatenate([jnp.concatenate([r, -i], 1), jnp.concatenate([i, r], 1)], 0)

        def tall(n):
            return jnp.concatenate([y_table[n, :, :512], y_table[n, :, 512:]], 0)

        out = product((arrange(re[0], im[0]), arrange(re[1], im[1])), (tall(0), tall(1)))
        cos, sin = y_twist[0], y_twist[1]

        def turned(slot, comp, want_im):
            a = out[lane(slot, comp, 0) : lane(slot, comp, 8)]
            if slot == 0:
                return a, None
            b = out[128 + lane(slot, comp, 0) : 128 + lane(slot, comp, 8)]
            c, s = cos[slot : slot + 1], sin[slot : slot + 1]
            return a * c - b * s, (b * c + a * s) if want_im else None

        field = []
        for comp in range(3):
            base = turned(0, comp, False)[0] + turned(4, comp, False)[0]
            one_re, one_im = turned(1, comp, True)
            two_re, _ = turned(2, comp, False)
            three_re, three_im = turned(3, comp, True)
            up, down = base + two_re, base - two_re
            re_sum, im_dif = one_re + three_re, one_im - three_im
            field.append([up + re_sum, down - im_dif, up - re_sum, down + im_dif])
        return field

    def x_transform(re, im, sign):
        re_high, re_low = halves(re)
        im_high, im_low = halves(im)

        def arrange(r, i):
            if sign < 0:
                return jnp.concatenate([jnp.concatenate([r, i], 1), jnp.concatenate([i, -r], 1)], 0)
            return jnp.concatenate([jnp.concatenate([r, i], 1), jnp.concatenate([-i, r], 1)], 0)

        out = product(
            (x_table[0], x_table[1]), (arrange(re_high, im_high), arrange(re_low, im_low))
        )
        return out[:, :128], out[:, 128:]

    def twist(re, im, sign):
        cos, sin = x_twist[0], x_twist[1]
        if sign < 0:
            return re * cos + im * sin, im * cos - re * sin
        return re * cos - im * sin, im * cos + re * sin

    def x_forward(turn_at):
        re, im = x_transform(recv[turn_at][:, 0, :], recv[turn_at][:, 1, :], -1)
        re, im = twist(re, im, -1)
        out = product(halves(jnp.concatenate([re, im], 1)), (eights[0, 0], eights[0, 1]))
        return out[:, :128], out[:, 128:]

    def x_inverse(re, im):
        out = product(halves(jnp.concatenate([re, im], 1)), (eights[1, 0], eights[1, 1]))
        re, im = twist(out[:, :128], out[:, 128:], 1)
        return x_transform(re, im, 1)

    for name in ("slip_rate", "y_twist", "y_table"):
        loads[name].wait()
    put(0, *y_forward([slip_rate[comp] for comp in range(3)]))

    def live(band, lag, comp):
        kept = (band_len[band] > lag).astype(F32)
        return kern[comp, band, lag] * kept

    effective = {
        (band, lag, comp): live(band, lag, comp)
        for lag in (0, 1, 2, 3) for comp in range(3) for band in range(BANDS)
    }
    effective.update({(0, lag, comp): live(0, lag, comp) for lag in range(4, LAGS) for comp in range(3)})

    for name in ("mode_band", "history", "past", "x_twist", "x_table"):
        loads[name].wait()

    def gather(mode, carry):
        at = pl.multiple_of(mode * 256, 256)
        band = mode_band[:, pl.ds(at, 256)]
        chosen = [band == b for b in range(BANDS)]
        for comp in range(3):
            total = [jnp.zeros((8, 256), F32), jnp.zeros((8, 256), F32)]
            for lag in range(2, LAGS):
                weight = jnp.zeros((8, 256), F32)
                for b in range(BANDS if lag < 4 else 1):
                    weight = jnp.where(chosen[b], effective[b, lag, comp], weight)
                for part in range(2):
                    source = history[lag - 2, comp, part, :, pl.ds(at, 256)].astype(F32)
                    total[part] = total[part] + weight * source
            for part in range(2):
                row = pl.multiple_of(((comp * 2 + part) * 8 + mode) * 8, 8)
                stacked[pl.ds(row, 8), :] = total[part]
        row = pl.multiple_of(mode * 8, 8)
        bands[pl.ds(row, 8), :] = band.astype(F32)
        return carry

    lax.fori_loop(0, 8, gather, 0)
    flat = halves(stacked[...].T)
    out = product(flat, (past[0], past[1]))
    sign = 1.0 - 2.0 * half.astype(F32)
    held_re, held_im = x_transform(*twist(out[:, :128], out[:, 128:256], 1), 1)
    hold[0] = held_re
    hold[1] = held_im * sign
    rest_re, rest_im = twist(out[:, 256:384], out[:, 384:], 1)
    rest_re, rest_im = halves(rest_re), halves(rest_im)
    rest = product(
        (x_table[0], x_table[1]),
        tuple(jnp.concatenate([rest_re[n], -rest_im[n]], 0) for n in range(2)),
    )
    lane_at = lax.broadcasted_iota(jnp.int32, (1, 128), 1)
    send_4[:, 0, :] = rest * jnp.where(lane_at < 64, 1.0, sign)

    pl.semaphore_wait(barrier, DEV - 1)
    band_copy = pltpu.make_async_remote_copy(
        mode_band.at[pl.ds(4, 4)], partner_band.at[pl.ds(4, 4)], pair_send.at[0], pair_recv.at[0],
        device_id=partner_id, device_id_type=MESH,
    )
    band_copy.start()
    exchange(0, True)
    exchange(4, False)
    for name in ("turn", "picks", "missing", "eights", "slip_field", "prestress"):
        loads[name].wait()

    band_copy.wait()
    for mode in range(8):
        bands[64 + mode * 8 : 72 + mode * 8, :] = partner_band[:, mode * 256 : (mode + 1) * 256].astype(F32)
    plain = bands[...].T.astype(BF16)
    dot = functools.partial(lax.dot_general, dimension_numbers=NN, preferred_element_type=F32)
    turned = dot(turn[...], plain).astype(BF16)
    first_row = lax.broadcasted_iota(jnp.int32, (256, 128), 0) == 0
    plain_band = dot(plain, picks[0]) + missing[0, 0:1]
    turned_band = (
        jnp.where(first_row, dot(turned, picks[2]), dot(turned, picks[1]))
        + missing[1, 0:1]
    )
    lane_comp = lax.rem(lane_at // 8, 3)
    weight = [jnp.zeros((256, 128), F32) for _ in range(2)]
    for which in (plain_band, turned_band):
        chosen = [jnp.zeros((256, 128), F32) for _ in range(2)]
        for b in range(BANDS):
            hit = which == float(b)
            for lag in range(2):
                value = jnp.where(
                    lane_comp == 0, effective[b, lag, 0],
                    jnp.where(lane_comp == 1, effective[b, lag, 1], effective[b, lag, 2]),
                )
                chosen[lag] = jnp.where(hit, value, chosen[lag])
        weight = [weight[lag] + chosen[lag] for lag in range(2)]
    first_weight = weight[0] + weight[1]
    now_weight = weight[1] + 0.5 * weight[0]
    tried_weight = 0.5 * weight[0]

    coeff = weakening(slip_field[0], slip_field[1])

    arrive(0)
    now_re, now_im = x_forward(0)
    re, im = x_inverse(now_re * first_weight, now_im * first_weight)
    put(1, re + hold[0], im + hold[1])
    exchange(1, False)
    re, im = x_inverse(now_re * now_weight, now_im * now_weight)
    hold[0] = re + hold[0]
    hold[1] = im + hold[1]
    arrive(4)
    rest = recv[4][:, 0, :].T
    kept[0, 0:64] = swap(rest[0:64])
    kept[1, 0:64] = swap(rest[64:128])
    arrive(1)
    field = y_inverse(1)
    stress = [prestress[comp] + jnp.concatenate(field[comp], 1) for comp in range(3)]

    put(2, *y_forward(slide(stress, coeff)))
    exchange(2, True)
    arrive(2)
    re, im = x_forward(2)
    re, im = x_inverse(re * tried_weight, im * tried_weight)
    put(3, re + hold[0], im + hold[1])
    exchange(3, False)
    arrive(3)
    field = y_inverse(3)
    for comp in range(3):
        for n in range(4):
            part = slice(512 * n, 512 * (n + 1))
            stress_out[comp, :, part] = prestress[comp, :, part] + field[comp][n]
    for turn_at in range(5):
        sent(turn_at)


def finish(stress, slip_field, slip_rate, new_rate, new_slip):
    coeff = weakening(slip_field[0], slip_field[1])
    for comp, value in enumerate(slide([stress[comp] for comp in range(3)], coeff)):
        new_rate[comp] = value
        new_slip[comp] = slip_field[comp] + 0.25 * (slip_rate[comp] + value)


def on_device(slip_rate, slip_field, prestress, history, kernel, band_len, mode_band):
    vmem = pl.BlockSpec(memory_space=pltpu.VMEM)
    smem = pl.BlockSpec(memory_space=pltpu.SMEM)
    anywhere = pl.BlockSpec(memory_space=pltpu.HBM)
    constants = [jnp.asarray(table) for table in tables()]
    halved = (5, 6, 7)
    shape = jax.ShapeDtypeStruct((3, 8, N), F32)
    dma = pltpu.SemaphoreType.DMA
    inputs = (slip_rate, slip_field, prestress, history, mode_band)
    stress = pl.pallas_call(
        body,
        out_shape=shape,
        in_specs=[anywhere] * (5 + len(constants)) + [smem] * 2,
        out_specs=vmem,
        scratch_shapes=[
            *[pltpu.VMEM(value.shape, value.dtype) for value in inputs],
            *[
                pltpu.VMEM(value.shape[1:] if at in halved else value.shape, value.dtype)
                for at, value in enumerate(constants)
            ],
            *[pltpu.VMEM((DEV, rows, 128), F32) for rows in (2, 2, 2, 2, 1) * 2],
            pltpu.VMEM((384, 256), F32),
            pltpu.VMEM((128, 256), F32),
            pltpu.VMEM((2, 256, 128), F32),
            pltpu.VMEM((2, 72, 256), F32),
            pltpu.VMEM((8, N), jnp.int32),
            dma((5,)), dma((5,)), dma((1,)), dma((1,)), dma((14,)),
        ],
        compiler_params=pltpu.CompilerParams(
            collective_id=0, has_side_effects=True, vmem_limit_bytes=62 * 1024 * 1024
        ),
    )(*inputs, *constants, jnp.transpose(kernel, (2, 0, 1)), band_len)
    return pl.pallas_call(
        finish, out_shape=(shape, shape), in_specs=[vmem] * 3, out_specs=(vmem, vmem),
        compiler_params=pltpu.CompilerParams(vmem_limit_bytes=4 * 1024 * 1024),
    )(stress, slip_field, slip_rate)


def solution(mesh):
    rows = P(None, ("kx", "ky"), None)
    return jax.shard_map(
        on_device,
        mesh=mesh,
        in_specs=(
            rows, rows, rows, P(None, None, None, ("kx", "ky"), None), P(), P(), P(("kx", "ky"), None),
        ),
        out_specs=(rows, rows),
        check_vma=False,
    )
```
